32 devices in a mesh: dp: 8 (over z, core), tensor: 4 (over y, x).
Axes of the slice: x: 2, y: 2, z: 4, core: 2. Of those that a mesh axis runs over, the one named last changes fastest.
Arguments:
- inputs: float32 [13848, 1024], P('dp'), may hold values from -6 to 6
- grad_out: float32 [13848, 1024], P('dp'), may hold values from -6 to 6
- w_qkv: bfloat16 [2, 3, 1024, 1024], P(None, None, 'dp', 'tensor'), may hold values from -0.1875 to 0.1875
- b_qv: bfloat16 [2, 2, 16, 64], P(None, None, 'tensor', 'dp'), may hold values from -3 to 3
- w_out: bfloat16 [2, 1024, 1024], P(None, 'tensor', 'dp'), may hold values from -0.75 to 0.75
- w_up: bfloat16 [2, 1024, 4096], P(None, 'dp', 'tensor'), may hold values from -0.1875 to 0.1875
- b_up: bfloat16 [2, 64, 64], P(None, 'tensor', 'dp'), may hold values from -3 to 3
- w_down: bfloat16 [2, 4096, 1024], P(None, 'tensor', 'dp'), may hold values from -0.09375 to 0.09375
- ln_gain: float32 [2, 2, 1024], P(None, None, ('dp', 'tensor')), may hold values from 0.1 to 1.9
- tok_bias: float32 [2, 4, 1024], P(None, None, ('dp', 'tensor')), may hold values from -3 to 3
Outputs:
- block_out: float32 [13848, 1024], P('dp')
- grad_in: float32 [13848, 1024], P('dp')
- grad_w_qkv: float32 [2, 3, 1024, 1024], P(None, None, 'dp', 'tensor')
- grad_b_qv: float32 [2, 2, 16, 64], P(None, None, 'tensor', 'dp')
- grad_w_out: float32 [2, 1024, 1024], P(None, 'tensor', 'dp')
- grad_w_up: float32 [2, 1024, 4096], P(None, 'dp', 'tensor')
- grad_b_up: float32 [2, 64, 64], P(None, 'tensor', 'dp')
- grad_w_down: float32 [2, 4096, 1024], P(None, 'tensor', 'dp')
- grad_ln_gain: float32 [2, 2, 1024], P(None, None, ('dp', 'tensor'))
- grad_tok_bias: float32 [2, 4, 1024], P(None, None, ('dp', 'tensor'))
The draws below stay inside these ranges and needn't reach their ends.
All inputs are finite; a program needn't handle non-finite values.
Results may differ from the reference program's by a relative error of at most 0.02.
Values may be sent and summed in bfloat16 or wider, within the bound.
No kernel may reach another device: no remote copies, remote signals or barrier semaphores. Data moves between devices by JAX's collectives and lax.ppermute only.
A program may use at most 256 MiB of HBM per device.

```python
import jax
import jax.numpy as jnp
from jax import lax

D = 1024
HEADS = 16
HEAD_DIM = 64
FF = 4096
SEQ = 577
LAYERS = 2
TOKENS = 13848
N_DP = 8


def shard_levels(rng, shape, split, smallest, largest):
    loudness, own = 1.0, jax.random.fold_in(rng, 6)
    for position, shards_of in split:
        heights = jnp.exp(jax.random.uniform(jax.random.fold_in(own, position), (shards_of,), jnp.float32, smallest / len(split), largest / len(split)))
        loudness = loudness * jnp.repeat(heights, shape[position] // shards_of).reshape([-1 if axis == position else 1 for axis in range(len(shape))])
    return loudness


def gaussian(key, dims, deviation, reach, pieces=(), kind=jnp.bfloat16):
    entries = jax.random.normal(key, dims, jnp.float32) * deviation
    if len(pieces) > 0:
        entries = shard_levels(key, dims, pieces, -0.22, 0.18) * entries
    return jnp.clip(entries, min=-reach, max=reach).astype(kind)


def setup_inputs(seed: int = 0) -> dict:
    arg_keys = jax.random.split(jax.random.key(seed), 11)
    return {
        "inputs": gaussian(arg_keys[0], (TOKENS, D), 1.0, 6.0, ((0, 8),), jnp.float32),
        "grad_out": gaussian(arg_keys[1], (TOKENS, D), 1.0, 6.0, ((0, 8),), jnp.float32),
        "w_qkv": gaussian(arg_keys[2], (LAYERS, 3, D, D), D ** -0.5, 0.1875, ((2, 8), (3, 4))),
        "b_qv": gaussian(arg_keys[3], (LAYERS, 2, HEADS, HEAD_DIM), 0.5, 3.0, ((2, 4), (3, 8))),
        "w_out": gaussian(arg_keys[4], (LAYERS, D, D), (D // 16) ** -0.5, 0.75, ((1, 4), (2, 8))),
        "w_up": gaussian(arg_keys[5], (LAYERS, D, FF), D ** -0.5, 0.1875, ((1, 8), (2, 4))),
        "b_up": gaussian(arg_keys[6], (LAYERS, FF // 64, 64), 0.5, 3.0, ((1, 4), (2, 8))),
        "w_down": gaussian(arg_keys[7], (LAYERS, FF, D), FF ** -0.5, 0.09375, ((1, 4), (2, 8))),
        "ln_gain": jnp.clip(1.0 + 0.18 * jax.random.normal(arg_keys[8], (LAYERS, 2, D), jnp.float32), 0.1, 1.9),
        "tok_bias": gaussian(arg_keys[9], (LAYERS, 4, D), 0.5, 3.0, ((2, 32),), jnp.float32),
    }


epsilon = 1e-05
root_half = 0.7071067811865476
inv_root_two_pi = 0.3989422804014327

def rounded(values):
    return lax.optimization_barrier(values.astype(jnp.bfloat16)).astype(jnp.float32)

def norm_forward(stream_rows, gain_row, shift_row):
    center = stream_rows - lax.optimization_barrier(jnp.mean(stream_rows, axis=-1, keepdims=True))
    inverse = lax.rsqrt(lax.optimization_barrier(jnp.mean(center * center, axis=-1, keepdims=True)) + epsilon)
    normed = center * inverse
    return (normed * gain_row + shift_row, normed, inverse)

def norm_backward(upstream, gain_row, normed, inverse):
    scaled = upstream * gain_row
    mean_one = lax.optimization_barrier(jnp.mean(scaled, axis=-1, keepdims=True))
    mean_two = lax.optimization_barrier(jnp.mean(scaled * normed, axis=-1, keepdims=True))
    return (inverse * (scaled - mean_one - normed * mean_two), lax.optimization_barrier(jnp.sum(upstream * normed, axis=0)), lax.optimization_barrier(jnp.sum(upstream, axis=0)))

def gelu_value(hidden):
    return hidden * (0.5 * (1.0 + lax.erf(hidden * root_half)))

def gelu_slope(hidden):
    return 0.5 * (1.0 + lax.erf(hidden * root_half)) + hidden * jnp.exp(-0.5 * hidden * hidden) * inv_root_two_pi

def attend_image(inputs):
    query_rows, key_rows, value_rows = inputs
    scores = jnp.einsum('qhd,khd->hqk', query_rows.astype(jnp.float32), key_rows.astype(jnp.float32))
    row_peak = lax.optimization_barrier(jnp.max(scores, axis=-1, keepdims=True))
    exponent = jnp.exp(scores - row_peak)
    totals = lax.optimization_barrier(jnp.sum(exponent, axis=-1, keepdims=True))
    attn_probs = rounded(exponent / totals)
    mixed_heads = jnp.einsum('hqk,khd->qhd', attn_probs, value_rows.astype(jnp.float32))
    return (mixed_heads.astype(jnp.bfloat16), (row_peak + jnp.log(totals))[..., 0])

def attend_back(inputs):
    query_rows, key_rows, value_rows, log_total, grad_mixed = inputs
    query_f = query_rows.astype(jnp.float32)
    key_f = key_rows.astype(jnp.float32)
    value_f = value_rows.astype(jnp.float32)
    mixed_f = grad_mixed.astype(jnp.float32)
    scores = jnp.einsum('qhd,khd->hqk', query_f, key_f)
    attn_probs = jnp.exp(scores - log_total[..., None])
    grad_probs = jnp.einsum('qhd,khd->hqk', mixed_f, value_f)
    inner_sum = lax.optimization_barrier(jnp.sum(attn_probs * grad_probs, axis=-1, keepdims=True))
    grad_scores = rounded(attn_probs * (grad_probs - inner_sum))
    grad_query = jnp.einsum('hqk,khd->qhd', grad_scores, key_f) * HEAD_DIM ** (-0.5)
    grad_key = jnp.einsum('hqk,qhd->khd', grad_scores, query_f)
    grad_value = jnp.einsum('hqk,qhd->khd', rounded(attn_probs), mixed_f)
    return jnp.stack([grad_query, grad_key, grad_value], axis=1)

def run_group(weights, rows_in, cot_in):
    w_qkv, b_qv, w_out, w_up, b_up, w_down, ln_gain, tok_bias = weights
    images = rows_in.shape[0] // SEQ
    image_shape = (images, SEQ, HEADS, HEAD_DIM)
    score_scale = HEAD_DIM ** (-0.5)
    stream = rows_in
    saved_list = []
    for block_index in range(LAYERS):
        qkv_w = w_qkv[block_index].astype(jnp.float32)
        normed_one, hat_one, inv_one = norm_forward(stream, ln_gain[block_index, 0], tok_bias[block_index, 0])
        rows_one = rounded(normed_one)
        projected = jnp.einsum('td,jde->tje', rows_one, qkv_w)
        biases = b_qv[block_index].reshape(2, D).astype(jnp.float32)
        query_rows = rounded((projected[:, 0] + biases[0]) * score_scale)
        key_rows = rounded(projected[:, 1])
        value_rows = rounded(projected[:, 2] + biases[1])
        mixed_heads, log_total = lax.map(attend_image, (query_rows.reshape(image_shape), key_rows.reshape(image_shape), value_rows.reshape(image_shape)))
        mixed_heads = mixed_heads.reshape(-1, D).astype(jnp.float32)
        middle = stream + jnp.dot(mixed_heads, w_out[block_index].astype(jnp.float32)) + tok_bias[block_index, 1]
        normed_two, hat_two, inv_two = norm_forward(middle, ln_gain[block_index, 1], tok_bias[block_index, 2])
        rows_two = rounded(normed_two)
        hidden = jnp.dot(rows_two, w_up[block_index].astype(jnp.float32)) + b_up[block_index].reshape(-1).astype(jnp.float32)
        activation = rounded(gelu_value(hidden))
        stream = middle + jnp.dot(activation, w_down[block_index].astype(jnp.float32)) + tok_bias[block_index, 3]
        saved_list.append((rows_one, hat_one, inv_one, query_rows, key_rows, value_rows, log_total, mixed_heads, rows_two, hat_two, inv_two, hidden, activation))
    cotangent = cot_in
    per_layer = [None] * LAYERS
    for block_index in reversed(range(LAYERS)):
        rows_one, hat_one, inv_one, query_rows, key_rows, value_rows, log_total, mixed_heads, rows_two, hat_two, inv_two, hidden, activation = saved_list[block_index]
        qkv_w = w_qkv[block_index].astype(jnp.float32)
        shift_down = lax.optimization_barrier(jnp.sum(cotangent, axis=0))
        cot_rows = rounded(cotangent)
        grad_down = jnp.dot(activation.T, cot_rows)
        grad_hidden = jnp.dot(cot_rows, w_down[block_index].astype(jnp.float32).T) * gelu_slope(hidden)
        grad_upb = lax.optimization_barrier(jnp.sum(grad_hidden, axis=0))
        hidden_rows = rounded(grad_hidden)
        grad_up = jnp.dot(rows_two.T, hidden_rows)
        back_two = jnp.dot(hidden_rows, w_up[block_index].astype(jnp.float32).T)
        dstream, gain_two, shift_two = norm_backward(back_two, ln_gain[block_index, 1], hat_two, inv_two)
        cotangent = cotangent + dstream
        shift_out = lax.optimization_barrier(jnp.sum(cotangent, axis=0))
        cot_rows = rounded(cotangent)
        grad_outw = jnp.dot(mixed_heads.T, cot_rows)
        grad_mixed = rounded(jnp.dot(cot_rows, w_out[block_index].astype(jnp.float32).T))
        qkv_grads = lax.map(attend_back, (query_rows.reshape(image_shape), key_rows.reshape(image_shape), value_rows.reshape(image_shape), log_total, grad_mixed.reshape(image_shape)))
        qkv_grads = qkv_grads.reshape(-1, 3, D)
        grad_qv = jnp.stack([lax.optimization_barrier(jnp.sum(qkv_grads[:, 0], axis=0)), lax.optimization_barrier(jnp.sum(qkv_grads[:, 2], axis=0))]).reshape(2, HEADS, HEAD_DIM)
        qkv_rows = rounded(qkv_grads)
        grad_qkvw = jnp.einsum('td,tje->jde', rows_one, qkv_rows)
        back_one = jnp.einsum('tje,jde->td', qkv_rows, qkv_w)
        dstream, gain_one, shift_one = norm_backward(back_one, ln_gain[block_index, 0], hat_one, inv_one)
        cotangent = cotangent + dstream
        per_layer[block_index] = (grad_qkvw, grad_qv, grad_outw, grad_up, grad_upb.reshape(FF // 64, 64), grad_down, jnp.stack([gain_one, gain_two]), jnp.stack([shift_one, shift_out, shift_two, shift_down]))
    grads = tuple((jnp.stack([per_layer[block_index][member] for block_index in range(LAYERS)]) for member in range(8)))
    return (stream, cotangent, grads)

def reference(inputs, grad_out, w_qkv, b_qv, w_out, w_up, b_up, w_down, ln_gain, tok_bias):
    weights = (w_qkv, b_qv, w_out, w_up, b_up, w_down, ln_gain, tok_bias)
    rows_all = inputs.reshape(N_DP, -1, D)
    cots_all = grad_out.reshape(N_DP, -1, D)
    initial = tuple((jnp.zeros(array.shape, jnp.float32) for array in weights))

    def group_step(running, group_pair):
        out_rows, back_rows, grads = run_group(weights, group_pair[0], group_pair[1])
        return (tuple((accum_part + new_part for accum_part, new_part in zip(running, grads))), (out_rows, back_rows))
    totals, (out_all, back_all) = lax.scan(group_step, initial, (rows_all, cots_all))
    return (out_all.reshape(-1, D), back_all.reshape(-1, D), totals[0], totals[1], totals[2], totals[3], totals[4], totals[5], totals[6], totals[7])
```

```python
import jax
import jax.numpy as jnp
import numpy as np
from jax import lax
from jax.experimental import pallas as pl
from jax.experimental.layout import Layout, with_layout_constraint
from jax.experimental.pallas import tpu as pltpu
from jax.sharding import Mesh
from jax.sharding import PartitionSpec as P

HEAD_DIM = 64
SEQ = 577
LAYERS = 2


epsilon = 1e-05
root_half = 0.7071067811865476
inv_root_two_pi = 0.3989422804014327


def norm_forward(stream_rows, gain_row, shift_row):
    center = stream_rows - jnp.mean(stream_rows, axis=-1, keepdims=True)
    inverse = lax.rsqrt(jnp.mean(center * center, axis=-1, keepdims=True) + epsilon)
    normed = center * inverse
    return (normed * gain_row + shift_row, normed, inverse)


def norm_backward(upstream, gain_row, normed, inverse):
    scaled = upstream * gain_row
    mean_one = jnp.mean(scaled, axis=-1, keepdims=True)
    mean_two = jnp.mean(scaled * normed, axis=-1, keepdims=True)
    return (
        inverse * (scaled - mean_one - normed * mean_two),
        jnp.sum(upstream * normed, axis=0),
        jnp.sum(upstream, axis=0),
    )


def gelu_value(hidden):
    return hidden * (0.5 * (1.0 + lax.erf(hidden * root_half)))


def gelu_slope(hidden):
    return (
        0.5 * (1.0 + lax.erf(hidden * root_half))
        + hidden * jnp.exp(-0.5 * hidden * hidden) * inv_root_two_pi
    )


def attend_image(inputs):
    query_rows, key_rows, value_rows = inputs
    scores = jnp.einsum("qhd,khd->hqk", query_rows, key_rows, preferred_element_type=jnp.float32)
    row_peak = jnp.max(scores, axis=-1, keepdims=True)
    exponent = jnp.exp(scores - row_peak)
    totals = jnp.sum(exponent, axis=-1, keepdims=True)
    attn_probs = (exponent / totals).astype(jnp.bfloat16)
    mixed_heads = jnp.einsum(
        "hqk,khd->qhd", attn_probs, value_rows, preferred_element_type=jnp.float32
    )
    return (mixed_heads.astype(jnp.bfloat16), (row_peak + jnp.log(totals))[..., 0])


def attend_back(inputs):
    query_rows, key_rows, value_rows, log_total, grad_mixed = inputs
    scores = jnp.einsum("qhd,khd->hqk", query_rows, key_rows, preferred_element_type=jnp.float32)
    attn_probs = jnp.exp(scores - log_total[..., None])
    grad_probs = jnp.einsum(
        "qhd,khd->hqk", grad_mixed, value_rows, preferred_element_type=jnp.float32
    )
    inner_sum = jnp.sum(attn_probs * grad_probs, axis=-1, keepdims=True)
    grad_scores = (attn_probs * (grad_probs - inner_sum)).astype(jnp.bfloat16)
    grad_query = jnp.einsum(
        "hqk,khd->qhd", grad_scores, key_rows, preferred_element_type=jnp.float32
    ) * HEAD_DIM ** (-0.5)
    grad_key = jnp.einsum(
        "hqk,qhd->khd", grad_scores, query_rows, preferred_element_type=jnp.float32
    )
    grad_value = jnp.einsum(
        "hqk,qhd->khd",
        attn_probs.astype(jnp.bfloat16),
        grad_mixed,
        preferred_element_type=jnp.float32,
    )
    return jnp.stack([grad_query, grad_key, grad_value], axis=1)


def fetch_forward(qkv_part, qv_part, out_part, up_part, upb_part, down_part):
    return (
        lax.all_gather(qkv_part, "dp", axis=1, tiled=True),
        lax.all_gather(qv_part, "dp", axis=2, tiled=True),
        lax.all_gather(out_part, "dp", axis=1, tiled=True),
        lax.all_gather(up_part, "dp", axis=0, tiled=True),
        lax.all_gather(upb_part, "dp", axis=1, tiled=True),
        lax.all_gather(down_part, "dp", axis=1, tiled=True),
    )


def fetch_again(qkv_part, qv_part, out_part, up_part, upb_part, down_part):
    return (
        lax.all_gather(qkv_part, "dp", axis=1, tiled=True),
        lax.all_gather(qv_part, "dp", axis=2, tiled=True),
        lax.all_gather(out_part, "dp", axis=1, tiled=True),
        lax.all_gather(up_part, "dp", axis=0, tiled=True),
        lax.all_gather(upb_part, "dp", axis=1, tiled=True),
        lax.all_gather(down_part, "dp", axis=1, tiled=True),
    )


def pad_rows(rows, extra_rows):
    return jnp.pad(rows, ((0, extra_rows), (0, 0)))


def spread_rows(token_rows, group_rows):
    return lax.all_gather(token_rows, "tensor", axis=0, tiled=True)[:group_rows]


def gather_cotangent(token_rows, group_rows):
    return lax.all_gather(token_rows, "tensor", axis=0, tiled=True)[:group_rows]


def reduce_branch(partial_rows, extra_rows):
    return lax.psum_scatter(
        pad_rows(partial_rows, extra_rows).astype(jnp.bfloat16),
        "tensor",
        scatter_dimension=0,
        tiled=True,
    ).astype(jnp.float32)


def branch_output(local_rows, local_w, extra_rows):
    return reduce_branch(
        jnp.dot(local_rows, local_w, preferred_element_type=jnp.float32), extra_rows
    )


def reduce_input(partial_rows, extra_rows):
    return lax.psum_scatter(
        pad_rows(partial_rows, extra_rows).astype(jnp.bfloat16),
        "tensor",
        scatter_dimension=0,
        tiled=True,
    ).astype(jnp.float32)


def reduce_weights(grad_qkvw, grad_qv, grad_outw, grad_up, grad_upb, grad_down):
    return (
        lax.psum_scatter(
            grad_qkvw.astype(jnp.bfloat16), "dp", scatter_dimension=1, tiled=True
        ).astype(jnp.float32),
        lax.psum_scatter(
            grad_qv.astype(jnp.bfloat16), "dp", scatter_dimension=2, tiled=True
        ).astype(jnp.float32),
        lax.psum_scatter(
            grad_outw.astype(jnp.bfloat16), "dp", scatter_dimension=1, tiled=True
        ).astype(jnp.float32),
        lax.psum_scatter(
            grad_up.astype(jnp.bfloat16), "dp", scatter_dimension=0, tiled=True
        ).astype(jnp.float32),
        lax.psum_scatter(
            grad_upb.astype(jnp.bfloat16), "dp", scatter_dimension=1, tiled=True
        ).astype(jnp.float32),
        lax.psum_scatter(
            grad_down.astype(jnp.bfloat16), "dp", scatter_dimension=1, tiled=True
        ).astype(jnp.float32),
    )


def shards(inputs, grad_out, w_qkv, b_qv, w_out, w_up, b_up, w_down, ln_gain, tok_bias):
    gains, shifts = (
        lax.all_gather(ln_gain, ("dp", "tensor"), axis=2, tiled=True),
        lax.all_gather(tok_bias, ("dp", "tensor"), axis=2, tiled=True),
    )
    score_scale = HEAD_DIM ** (-0.5)
    group_rows = inputs.shape[0]
    tensor_count = lax.axis_size("tensor")
    share_rows = (group_rows + tensor_count - 1) // tensor_count
    extra_rows = share_rows * tensor_count - group_rows
    row_offset = lax.axis_index("tensor") * share_rows
    images = group_rows // SEQ
    stream = lax.dynamic_slice_in_dim(pad_rows(inputs, extra_rows), row_offset, share_rows, 0)
    cotangent = lax.dynamic_slice_in_dim(pad_rows(grad_out, extra_rows), row_offset, share_rows, 0)
    saved_list = []
    for block_index in range(LAYERS):
        fetched = fetch_forward(
            w_qkv[block_index],
            b_qv[block_index],
            w_out[block_index],
            w_up[block_index],
            b_up[block_index],
            w_down[block_index],
        )
        qkv_w, qv_bias, out_w, up_w, up_bias, down_w = fetched
        local_width = qkv_w.shape[2]
        image_shape = (images, SEQ, local_width // HEAD_DIM, HEAD_DIM)
        normed_one, hat_one, inv_one = norm_forward(
            stream, gains[block_index, 0], shifts[block_index, 0]
        )
        rows_one = normed_one.astype(jnp.bfloat16)
        whole_one = spread_rows(rows_one, group_rows)
        projected = jnp.einsum("td,jde->tje", whole_one, qkv_w, preferred_element_type=jnp.float32)
        biases = qv_bias.reshape(2, local_width).astype(jnp.float32)
        query_rows = ((projected[:, 0] + biases[0]) * score_scale).astype(jnp.bfloat16)
        key_rows = projected[:, 1].astype(jnp.bfloat16)
        value_rows = (projected[:, 2] + biases[1]).astype(jnp.bfloat16)
        mixed_heads, log_total = lax.map(
            attend_image,
            (
                query_rows.reshape(image_shape),
                key_rows.reshape(image_shape),
                value_rows.reshape(image_shape),
            ),
        )
        mixed_heads = mixed_heads.reshape(-1, local_width)
        middle = stream + branch_output(mixed_heads, out_w, extra_rows) + shifts[block_index, 1]
        normed_two, hat_two, inv_two = norm_forward(
            middle, gains[block_index, 1], shifts[block_index, 2]
        )
        rows_two = normed_two.astype(jnp.bfloat16)
        whole_two = spread_rows(rows_two, group_rows)
        hidden = jnp.dot(whole_two, up_w, preferred_element_type=jnp.float32) + up_bias.reshape(
            -1
        ).astype(jnp.float32)
        activation = gelu_value(hidden).astype(jnp.bfloat16)
        stream = middle + branch_output(activation, down_w, extra_rows) + shifts[block_index, 3]
        saved_list.append(
            (
                fetched,
                rows_one,
                whole_one,
                hat_one,
                inv_one,
                query_rows,
                key_rows,
                value_rows,
                log_total,
                mixed_heads,
                rows_two,
                whole_two,
                hat_two,
                inv_two,
                hidden,
                activation,
            )
        )
    weight_list = [None] * LAYERS
    gain_list = [None] * LAYERS
    shift_list = [None] * LAYERS
    for block_index in reversed(range(LAYERS)):
        (
            fetched,
            rows_one,
            whole_one,
            hat_one,
            inv_one,
            query_rows,
            key_rows,
            value_rows,
            log_total,
            mixed_heads,
            rows_two,
            whole_two,
            hat_two,
            inv_two,
            hidden,
            activation,
        ) = saved_list[block_index]
        qkv_w, qv_bias, out_w, up_w, up_bias, down_w = fetch_again(
            w_qkv[block_index],
            b_qv[block_index],
            w_out[block_index],
            w_up[block_index],
            b_up[block_index],
            w_down[block_index],
        )
        local_width = qkv_w.shape[2]
        local_heads = local_width // HEAD_DIM
        image_shape = (images, SEQ, local_heads, HEAD_DIM)
        shift_down = jnp.sum(cotangent, axis=0)
        whole_cot = gather_cotangent(cotangent.astype(jnp.bfloat16), group_rows)
        grad_down = jnp.einsum(
            "tf,td->fd", activation, whole_cot, preferred_element_type=jnp.float32
        )
        grad_hidden = jnp.einsum(
            "td,fd->tf", whole_cot, down_w, preferred_element_type=jnp.float32
        ) * gelu_slope(hidden)
        grad_upb = jnp.sum(grad_hidden, axis=0)
        hidden_rows = grad_hidden.astype(jnp.bfloat16)
        grad_up = jnp.einsum(
            "td,tf->df", whole_two, hidden_rows, preferred_element_type=jnp.float32
        )
        back_two = reduce_input(
            jnp.einsum("tf,df->td", hidden_rows, up_w, preferred_element_type=jnp.float32),
            extra_rows,
        )
        dstream, gain_two, shift_two = norm_backward(
            back_two, gains[block_index, 1], hat_two, inv_two
        )
        cotangent = cotangent + dstream
        shift_out = jnp.sum(cotangent, axis=0)
        whole_cot = gather_cotangent(cotangent.astype(jnp.bfloat16), group_rows)
        grad_outw = jnp.einsum(
            "te,td->ed", mixed_heads, whole_cot, preferred_element_type=jnp.float32
        )
        grad_mixed = jnp.einsum(
            "td,ed->te", whole_cot, out_w, preferred_element_type=jnp.float32
        ).astype(jnp.bfloat16)
        qkv_grads = lax.map(
            attend_back,
            (
                query_rows.reshape(image_shape),
                key_rows.reshape(image_shape),
                value_rows.reshape(image_shape),
                log_total,
                grad_mixed.reshape(image_shape),
            ),
        )
        qkv_grads = qkv_grads.reshape(-1, 3, local_width)
        grad_qv = jnp.stack(
            [jnp.sum(qkv_grads[:, 0], axis=0), jnp.sum(qkv_grads[:, 2], axis=0)]
        ).reshape(2, local_heads, HEAD_DIM)
        qkv_rows = qkv_grads.astype(jnp.bfloat16)
        grad_qkvw = jnp.einsum(
            "td,tje->jde", whole_one, qkv_rows, preferred_element_type=jnp.float32
        )
        back_one = reduce_input(
            jnp.einsum("tje,jde->td", qkv_rows, qkv_w, preferred_element_type=jnp.float32),
            extra_rows,
        )
        dstream, gain_one, shift_one = norm_backward(
            back_one, gains[block_index, 0], hat_one, inv_one
        )
        cotangent = cotangent + dstream
        weight_list[block_index] = reduce_weights(
            grad_qkvw, grad_qv, grad_outw, grad_up, grad_upb.reshape(up_bias.shape), grad_down
        )
        gain_list[block_index] = jnp.stack([gain_one, gain_two])
        shift_list[block_index] = jnp.stack([shift_one, shift_out, shift_two, shift_down])
    gain_total, shift_total = (
        lax.psum_scatter(jnp.stack(gain_list), ("dp", "tensor"), scatter_dimension=2, tiled=True),
        lax.psum_scatter(jnp.stack(shift_list), ("dp", "tensor"), scatter_dimension=2, tiled=True),
    )
    full_out, full_back = (
        lax.all_gather(stream.astype(jnp.bfloat16), "tensor", axis=0, tiled=True).astype(
            stream.dtype
        ),
        lax.all_gather(cotangent.astype(jnp.bfloat16), "tensor", axis=0, tiled=True).astype(
            cotangent.dtype
        ),
    )
    stacked = [
        jnp.stack([weight_list[block_index][member] for block_index in range(LAYERS)])
        for member in range(6)
    ]
    return (
        full_out[:group_rows],
        full_back[:group_rows],
        stacked[0],
        stacked[1],
        stacked[2],
        stacked[3],
        stacked[4],
        stacked[5],
        gain_total,
        shift_total,
    )


CELLS = ("z", "core", "y", "x")
PHASES = {
    (1, 4): (("mlp", 1),),
    (0, 1): (("att", 1),),
    (0, 4): (("att", 1), ("mlp", 1)),
    (0, 5): (("mlp", 0),),
}
FLIP = ((0, 1), (1, 0))
TILE = 16
LANES = 128
NEGATIVE = -1e30
VMEM_LIMIT = 56 * 1024 * 1024


def round_up(count, multiple):
    return (count + multiple - 1) // multiple * multiple


WHOLE = round_up(SEQ, TILE)
PART_ROWS = (SEQ + 1) // 2
PART = round_up(PART_ROWS, TILE)
CHIP_ROWS = WHOLE + PART
SHARE = CHIP_ROWS // 2
SPILL = WHOLE - SHARE
NT = (((1,), (1,)), ((), ()))
TN = (((0,), (0,)), ((), ()))
NN = (((1,), (0,)), ((), ()))


def product(left, right, dims):
    return lax.dot_general(left, right, dims, preferred_element_type=jnp.float32)


def lane_pick(values, half):
    lane = lax.broadcasted_iota(jnp.int32, (1, values.shape[1]), 1)
    keep = lane < HEAD_DIM if half == 0 else lane >= HEAD_DIM
    return jnp.where(keep, values, jnp.zeros_like(values))


def whole_rows(ref, core):
    first = pl.multiple_of(core * SHARE, TILE)
    second = pl.multiple_of((1 - core) * SHARE, TILE)
    return jnp.concatenate([ref[pl.ds(first, SHARE), :], ref[pl.ds(second, SPILL), :]], axis=0)


def store_whole(ref, core, values, lanes):
    first = pl.multiple_of(core * SHARE, TILE)
    second = pl.multiple_of((1 - core) * SHARE, TILE)
    ref[pl.ds(first, SHARE), lanes] = values[:SHARE]
    ref[pl.ds(second, SPILL), lanes] = values[SHARE:]


def part_rows(ref, core):
    start = pl.multiple_of((1 - core) * SHARE + SPILL, TILE)
    return ref[pl.ds(start, PART), :]


def whole_keys():
    return lax.broadcasted_iota(jnp.int32, (WHOLE, 1), 0) < SEQ


def part_keys(mine):
    row = lax.broadcasted_iota(jnp.int32, (2 * PART, 1), 0)
    return (row < mine) | ((row >= PART) & (row < PART + SEQ - mine))


def attend_pair(query, key, value, good, lse_ref, slot):
    total = None
    for half in range(2):
        scores = product(lane_pick(key, half), query, NT)
        scores = jnp.where(good, scores, NEGATIVE)
        peak = jnp.max(scores, axis=0, keepdims=True)
        exponent = jnp.exp(scores - peak)
        sums = jnp.sum(exponent, axis=0, keepdims=True)
        probs = (exponent * (1.0 / sums)).astype(jnp.bfloat16)
        lse_ref[0, pl.ds(2 * slot + half, 1), :] = peak + jnp.log(sums)
        mixed = product(lane_pick(value, half), probs, TN)
        total = mixed if total is None else total + mixed
    return total.T.astype(jnp.bfloat16)


def attend_whole_kernel(place, qkv_a, qkv_b, mix_a, mix_b, lse_ref):
    core = place[0]
    good = whole_keys()
    for slot, (qkv, mix) in enumerate(((qkv_a, mix_a), (qkv_b, mix_b))):
        rows = whole_rows(qkv, core)
        mixed = attend_pair(
            rows[:, :LANES], rows[:, LANES : 2 * LANES], rows[:, 2 * LANES :], good, lse_ref, slot
        )
        store_whole(mix, core, mixed, slice(None))


def attend_part_kernel(place, qkv_a, qkv_b, far_a, far_b, mix_a, mix_b, lse_ref):
    core = place[0]
    good = part_keys(place[1])
    for slot, (qkv, far, mix) in enumerate(((qkv_a, far_a, mix_a), (qkv_b, far_b, mix_b))):
        rows = part_rows(qkv, core)
        key = jnp.concatenate([rows[:, LANES : 2 * LANES], far[:, :LANES]], axis=0)
        value = jnp.concatenate([rows[:, 2 * LANES :], far[:, LANES:]], axis=0)
        mix[...] = attend_pair(rows[:, :LANES], key, value, good, lse_ref, slot)


def attend_pair_back(query, key, value, upstream, good, lse_ref, slot):
    grad_key = grad_value = grad_query = None
    for half in range(2):
        lse = lse_ref[0, pl.ds(2 * slot + half, 1), :]
        key_half = lane_pick(key, half)
        scores = product(key_half, query, NT)
        probs = jnp.where(good, jnp.exp(scores - lse), 0.0)
        grad_probs = product(lane_pick(value, half), upstream, NT)
        inner = jnp.sum(probs * grad_probs, axis=0, keepdims=True)
        grad_scores = (probs * (grad_probs - inner)).astype(jnp.bfloat16)
        probs = probs.astype(jnp.bfloat16)
        some_key = product(grad_scores, lane_pick(query, half), NN)
        some_value = product(probs, lane_pick(upstream, half), NN)
        some_query = product(key_half, grad_scores, TN)
        grad_key = some_key if grad_key is None else grad_key + some_key
        grad_value = some_value if grad_value is None else grad_value + some_value
        grad_query = some_query if grad_query is None else grad_query + some_query
    return grad_query.T * HEAD_DIM ** (-0.5), grad_key, grad_value


def store_sums(sum_ref, slot, grad_query, grad_value):
    sum_ref[0, pl.ds(2 * slot, 1), :] = jnp.sum(grad_query, axis=0, keepdims=True)
    sum_ref[0, pl.ds(2 * slot + 1, 1), :] = jnp.sum(grad_value, axis=0, keepdims=True)


def back_whole_kernel(place, qkv_a, qkv_b, up_a, up_b, lse_ref, out_a, out_b, sum_ref):
    core = place[0]
    good = whole_keys()
    for slot, (qkv, up, out) in enumerate(((qkv_a, up_a, out_a), (qkv_b, up_b, out_b))):
        rows = whole_rows(qkv, core)
        grads = attend_pair_back(
            rows[:, :LANES],
            rows[:, LANES : 2 * LANES],
            rows[:, 2 * LANES :],
            whole_rows(up, core),
            good,
            lse_ref,
            slot,
        )
        store_sums(sum_ref, slot, grads[0], grads[2])
        for place_of, grad in enumerate(grads):
            lanes = slice(place_of * LANES, (place_of + 1) * LANES)
            store_whole(out, core, grad.astype(jnp.bfloat16), lanes)


def back_part_kernel(
    place, qkv_a, qkv_b, far_a, far_b, up_a, up_b, lse_ref, own_a, own_b, out_a, out_b, sum_ref
):
    core = place[0]
    good = part_keys(place[1])
    groups = ((qkv_a, far_a, up_a, own_a, out_a), (qkv_b, far_b, up_b, own_b, out_b))
    for slot, (qkv, far, up, own, out) in enumerate(groups):
        rows = part_rows(qkv, core)
        key = jnp.concatenate([rows[:, LANES : 2 * LANES], far[:, :LANES]], axis=0)
        value = jnp.concatenate([rows[:, 2 * LANES :], far[:, LANES:]], axis=0)
        grad_query, grad_key, grad_value = attend_pair_back(
            rows[:, :LANES], key, value, part_rows(up, core), good, lse_ref, slot
        )
        store_sums(sum_ref, slot, grad_query, grad_value)
        own[:, :LANES] = grad_query
        own[:, LANES : 2 * LANES] = grad_key[:PART]
        own[:, 2 * LANES :] = grad_value[:PART]
        out[:, :LANES] = grad_key[PART:].astype(jnp.bfloat16)
        out[:, LANES:] = grad_value[PART:].astype(jnp.bfloat16)


def by_pair(rows, lanes):
    return pl.BlockSpec((rows, lanes), lambda pair: (0, pair))


def stats(rows):
    return pl.BlockSpec((1, 8, rows), lambda pair: (pair, 0, 0))


def kernel_call(kernel, pairs, ins, in_specs, outs, out_specs):
    return pl.pallas_call(
        kernel,
        grid=(pairs,),
        in_specs=[pl.BlockSpec(memory_space=pltpu.SMEM)] + in_specs,
        out_specs=out_specs,
        out_shape=[jax.ShapeDtypeStruct(shape, kind) for shape, kind in outs],
        compiler_params=pltpu.CompilerParams(
            dimension_semantics=("arbitrary",), vmem_limit_bytes=VMEM_LIMIT
        ),
    )(*ins)


def attend_whole(place, qkv, pairs):
    mix = ((CHIP_ROWS, pairs * LANES), jnp.bfloat16)
    *mixed, lse = kernel_call(
        attend_whole_kernel,
        pairs,
        (place, *qkv),
        [by_pair(CHIP_ROWS, 3 * LANES)] * 2,
        [mix, mix, ((pairs, 8, WHOLE), jnp.float32)],
        [by_pair(CHIP_ROWS, LANES)] * 2 + [stats(WHOLE)],
    )
    return mixed, lse


def attend_part(place, qkv, far, pairs):
    mix = ((PART, pairs * LANES), jnp.bfloat16)
    *mixed, lse = kernel_call(
        attend_part_kernel,
        pairs,
        (place, *qkv, *far),
        [by_pair(CHIP_ROWS, 3 * LANES)] * 2 + [by_pair(PART, 2 * LANES)] * 2,
        [mix, mix, ((pairs, 8, PART), jnp.float32)],
        [by_pair(PART, LANES)] * 2 + [stats(PART)],
    )
    return mixed, lse


def back_whole(place, qkv, upstream, lse, pairs):
    out = ((CHIP_ROWS, 3 * pairs * LANES), jnp.bfloat16)
    *grads, sums = kernel_call(
        back_whole_kernel,
        pairs,
        (place, *qkv, *upstream, lse),
        [by_pair(CHIP_ROWS, 3 * LANES)] * 2
        + [by_pair(CHIP_ROWS, LANES)] * 2
        + [stats(WHOLE)],
        [out, out, ((pairs, 8, LANES), jnp.float32)],
        [by_pair(CHIP_ROWS, 3 * LANES)] * 2 + [stats(LANES)],
    )
    return grads, sums


def back_part(place, qkv, far, upstream, lse, pairs):
    own = ((PART, 3 * pairs * LANES), jnp.float32)
    out = ((PART, 2 * pairs * LANES), jnp.bfloat16)
    own_a, own_b, out_a, out_b, sums = kernel_call(
        back_part_kernel,
        pairs,
        (place, *qkv, *far, *upstream, lse),
        [by_pair(CHIP_ROWS, 3 * LANES)] * 2
        + [by_pair(PART, 2 * LANES)] * 2
        + [by_pair(CHIP_ROWS, LANES)] * 2
        + [stats(PART)],
        [own, own, out, out, ((pairs, 8, LANES), jnp.float32)],
        [by_pair(PART, 3 * LANES)] * 2 + [by_pair(PART, 2 * LANES)] * 2 + [stats(LANES)],
    )
    return (own_a, own_b), (out_a, out_b), sums


def give_kernel(place, round_00, round_01, round_10, round_11, out):
    y, x = place[2], place[3]
    near = [jnp.where(x == 0, a, b) for a, b in ((round_00[...], round_10[...]), (round_01[...], round_11[...]))]
    far = [jnp.where(x == 1, a, b) for a, b in ((round_00[...], round_10[...]), (round_01[...], round_11[...]))]
    row = 0
    tails = []
    for rounds in (near, far):
        whole = jnp.where(y == 0, rounds[0], rounds[1]).astype(jnp.float32)
        tail = jnp.where(y == 1, rounds[0], rounds[1]).astype(jnp.float32)
        out[row : row + SHARE, :] = whole
        out[row + SHARE : row + SEQ, :] = tail[: SEQ - SHARE]
        tails.append(tail)
        row += SEQ
    rest = SEQ - PART_ROWS
    out[row : row + PART_ROWS, :] = tails[0][SPILL : SPILL + PART_ROWS]
    out[row + PART_ROWS : row + SEQ, :] = tails[1][SPILL : SPILL + rest]


def give_call(place, rounds):
    width = rounds[0].shape[1]
    wide = 2 * LANES
    grid_spec = pltpu.PrefetchScalarGridSpec(
        num_scalar_prefetch=1,
        grid=(width // wide,),
        in_specs=[pl.BlockSpec((SHARE, wide), lambda col, place: (0, col))] * 4,
        out_specs=pl.BlockSpec((3 * SEQ, wide), lambda col, place: (0, col)),
    )
    return pl.pallas_call(
        give_kernel,
        grid_spec=grid_spec,
        out_shape=jax.ShapeDtypeStruct((3 * SEQ, width), jnp.float32),
        compiler_params=pltpu.CompilerParams(vmem_limit_bytes=VMEM_LIMIT),
        name="give_rows",
    )(place, *rounds)


def natural(values):
    return with_layout_constraint(values, Layout((0, 1)))


def tie(*values):
    return lax.optimization_barrier(values)


def cell_moves(sizes, target):
    moves = []
    index = {cell: number for number, cell in enumerate(np.ndindex(*sizes))}
    for cell, number in index.items():
        goal = target(*cell)
        if goal is not None:
            moves.append((number, index[goal]))
    return moves


def cells_body(sizes):
    n_z, _, _, _ = sizes
    trade = cell_moves(
        sizes, lambda z, c, y, x: (z, c, y, 1 - x) if c == 0 else (z, c, 1 - y, x)
    )
    relay_y = cell_moves(
        sizes, lambda z, c, y, x: (z, 1, 1 - y, x) if c == 0 else (z, 0, y, x)
    )
    relay_x = cell_moves(sizes, lambda z, c, y, x: (z, 1, y, 1 - x) if c == 1 else None)
    back_y = cell_moves(
        sizes, lambda z, c, y, x: (z, 0, 1 - y, x) if c == 1 else (z, 1, y, x)
    )
    lend = cell_moves(
        sizes, lambda z, c, y, x: (z, c, 1 - y, x) if c == y else (z, 1 - c, y, x)
    )
    repay = cell_moves(
        sizes, lambda z, c, y, x: (z, c, 1 - y, x) if c != y else (z, 1 - c, y, x)
    )
    images_axis = ("z", "core")
    chips = ("y", "x")

    def move(values, moves):
        return lax.ppermute(values, CELLS, moves)

    def spread(quarter, core):
        half = quarter.shape[0] // 2
        slot_a = move(quarter, trade)
        upper = move(slot_a[:half], relay_y)
        lower = move(slot_a[half:], relay_x)
        slot_b = jnp.where(core == 0, quarter, jnp.concatenate([upper, lower], axis=0))
        return slot_a, natural(slot_b)

    def collect_far(grad_b):
        half = grad_b.shape[0] // 2
        return (move(grad_b[:half], back_y), move(grad_b[half:], relay_x))

    def collect_near(grad_a, come, core):
        half = grad_a.shape[0] // 2
        come = jnp.where(core == 0, come[0], come[1])
        piece = lax.dynamic_slice(grad_a, (core * half, 0), come.shape)
        piece = (piece.astype(jnp.float32) + come.astype(jnp.float32)).astype(jnp.bfloat16)
        grad_a = lax.dynamic_update_slice(grad_a, piece, (core * half, 0))
        return move(grad_a, trade)

    def collect_end(grad_b, traded, home):
        if isinstance(grad_b, list):
            mine = [
                jnp.where(home, kept.astype(jnp.float32) + come.astype(jnp.float32), 0.0)
                for kept, come in zip(grad_b, traded)
            ]
            mine = jnp.concatenate([part.astype(jnp.bfloat16) for part in mine], axis=1)
        else:
            kept = jnp.where(home, grad_b.astype(jnp.float32), 0.0)
            mine = (kept + traded.astype(jnp.float32)).astype(jnp.bfloat16)
        return natural(mine)

    def collect_sum(mine):
        return lax.psum_scatter(mine, images_axis, scatter_dimension=0, tiled=True)

    def start_stream(grads, pack):
        return {"grads": grads, "pack": pack, "held": collect_far(grads[1]), "step": 0}

    def start_pair(grads, home, pack):
        held = [move(grad, repay) for grad in grads]
        return {"grads": (None, grads), "pack": pack, "held": held, "step": 1, "home": home}

    def advance(value, stream, core):
        value, held = tie(value, stream["held"])
        step = stream["step"]
        if step == 0:
            held = collect_near(stream["grads"][0], held, core)
        elif step == 1:
            home = stream.get("home", core == 0)
            value, held = tie(value, collect_end(stream["grads"][1], held, home))
            held = collect_sum(held)
        stream["held"], stream["step"] = held, step + 1
        return value

    def gather_quad(values):
        across = lax.ppermute(values, "x", FLIP)
        near = flip(values)
        far = flip(across)
        return jnp.concatenate([values, near, across, far], axis=0)

    def reduce_quad(left, right, dims):
        far = product(left[3 * SHARE :], right, dims).astype(jnp.bfloat16)
        far = flip(far)
        across = product(left[2 * SHARE : 3 * SHARE], right, dims)
        across = (across + far.astype(jnp.float32)).astype(jnp.bfloat16)
        across = lax.ppermute(across, "x", FLIP)
        near = product(left[SHARE : 2 * SHARE], right, dims).astype(jnp.bfloat16)
        near = flip(near)
        own = product(left[:SHARE], right, dims)
        return own + near.astype(jnp.float32) + across.astype(jnp.float32)

    def total_of(table):
        for axis in ("x", "y", "core"):
            come = lax.ppermute(table, axis, FLIP)
            table = table + come
        gap = 1
        while gap < n_z:
            if n_z % (2 * gap):
                return lax.psum(table, "z")
            partner = [(z, z ^ gap) for z in range(n_z)]
            table = table + lax.ppermute(table, "z", partner)
            gap *= 2
        return table

    def flip(values):
        return lax.ppermute(values, "core", FLIP)

    def both(values):
        return jnp.concatenate([values, flip(values)], axis=0)

    def reduce_pair(lefts, rights, dims):
        other = sum(
            product(left[SHARE:], right, dims) for left, right in zip(lefts, rights)
        )
        other = flip(other.astype(jnp.bfloat16))
        own = sum(product(left[:SHARE], right, dims) for left, right in zip(lefts, rights))
        return own + other.astype(jnp.float32)

    def share_of(rows, x, part):
        width = rows.shape[1]
        if part == 0:
            return lax.dynamic_slice(rows, (SEQ * x, 0), (SHARE, width))
        tail = lax.dynamic_slice(rows, (SEQ * x + SHARE, 0), (SEQ - SHARE, width))
        split = lax.dynamic_slice(
            rows, (2 * SEQ + PART_ROWS * x, 0), (SEQ - PART_ROWS, width)
        )
        last = rows[2 * SEQ + PART_ROWS - 1 : 2 * SEQ + PART_ROWS]
        last = jnp.where(x == 0, last, jnp.zeros_like(last))
        return jnp.concatenate(
            [
                tail,
                jnp.zeros((WHOLE - SEQ, width), rows.dtype),
                split,
                last,
                jnp.zeros((PART - PART_ROWS, width), rows.dtype),
            ],
            axis=0,
        )

    def take_share(rows, core, y, x):
        shares = share_of(rows, x, 0), share_of(rows, x, 1)
        own = jnp.where(core == 0, shares[0], shares[1])
        come = flip(jnp.where(core == 0, shares[1], shares[0]))
        return jnp.where(core == y, own, come)

    def share_rows(share, home):
        share = share.astype(jnp.bfloat16)
        rounds = []
        for number in range(4):
            dx, dc = divmod(number, 2)
            moves = cell_moves(
                sizes, lambda z, c, y, x, dx=dx, dc=dc: (z, y, c ^ dc, x ^ dx)
            )
            moves = [(a, b) for a, b in moves if a != b]
            come = move(share, moves)
            rounds.append(jnp.where(home, share, come) if number == 0 else come)
        return rounds

    def cells_step(inputs, grad_out, w_qkv, b_qv, w_out, w_up, b_up, w_down, ln_gain, tok_bias):
        core, y, x = (lax.axis_index(name) for name in ("core", "y", "x"))
        quarter_a = jnp.where(core == 0, 2 * y + 1 - x, 2 * (1 - y) + x)
        quarter_b = jnp.where(core == 0, 2 * y + x, 2 * (1 - y) + 1 - x)
        quarters = (quarter_a, quarter_b)
        place = jnp.stack([core, PART_ROWS - x, y, x]).astype(jnp.int32)
        width = inputs.shape[1]
        heads = b_qv.shape[2]
        local = heads * HEAD_DIM
        pairs = local // LANES
        units = w_up.shape[2]
        n_dp = 2 * n_z
        n_dev = 4 * n_dp
        piece = width // n_dev

        def pack_attention(layer):
            cols = [
                w_qkv[layer, member][:, pair * LANES : (pair + 1) * LANES]
                for pair in range(pairs)
                for member in range(3)
            ]
            return jnp.concatenate(cols + [w_out[layer].T], axis=1)

        packs = []
        for layer in range(LAYERS):
            packs += [pack_attention(layer), w_up[layer], w_down[layer].T]
        whole = []
        for pack in packs:
            whole.append(natural(lax.all_gather(natural(pack), images_axis, axis=0, tiled=True)))
        home = core == y
        weights = []
        for pack, quarter in enumerate(whole):
            if pack % 3 == 0:
                weights.append(spread(quarter, core))
            else:
                weights.append((quarter, move(quarter, lend)))

        small = jnp.concatenate(
            [
                ln_gain.reshape(-1, piece),
                tok_bias.reshape(-1, piece),
                b_qv.astype(jnp.float32).reshape(-1, piece),
                b_up.astype(jnp.float32).reshape(-1, piece),
            ],
            axis=0,
        )
        n_gain, n_bias, n_qv = 2 * LAYERS, 4 * LAYERS, b_qv.size // piece
        table = lax.all_gather(small, images_axis, axis=0)
        table = lax.all_gather(table, chips, axis=0)
        inputs, grad_out, table, _ = tie(inputs, grad_out, table, whole[0])
        stream = take_share(inputs, core, y, x)
        cotangent = take_share(grad_out, core, y, x)
        stream, cotangent = tie(stream, cotangent)
        first_rows = gather_quad(cotangent.astype(jnp.bfloat16))
        tokens = jnp.transpose(table[:, :, : n_gain + n_bias], (2, 1, 0, 3)).reshape(-1, width)
        gains = tokens[:n_gain].reshape(LAYERS, 2, width)
        shifts = tokens[n_gain:].reshape(LAYERS, 4, width)
        f_head = b_qv.shape[3]
        rows_up, f_up = b_up.shape[1], b_up.shape[2]
        head_bias = []
        for quarter in quarters:
            mine = lax.dynamic_index_in_dim(table, quarter, 0, keepdims=False)
            part = mine[:, n_gain + n_bias : n_gain + n_bias + n_qv]
            part = part.reshape(n_dp, LAYERS, 2, heads, f_head)
            head_bias.append(jnp.transpose(part, (1, 2, 3, 0, 4)).reshape(LAYERS, 2, local))
        up_quarter = 2 * core + x
        mine = lax.dynamic_index_in_dim(table, up_quarter, 0, keepdims=False)
        part = mine[:, n_gain + n_bias + n_qv :].reshape(n_dp, LAYERS, rows_up, f_up)
        up_bias = jnp.transpose(part, (1, 2, 0, 3)).reshape(LAYERS, 1, units)

        def qkv_bias(slot, layer):
            rows = head_bias[slot][layer].reshape(2, pairs, LANES)
            zero = jnp.zeros_like(rows[0])
            return jnp.stack([rows[0], zero, rows[1]], axis=1).reshape(1, -1)

        unit = jnp.ones((LANES,), jnp.float32)
        qkv_scale = jnp.tile(jnp.concatenate([unit * HEAD_DIM ** (-0.5), unit, unit]), pairs)
        part_start = jnp.where(core == 0, SHARE + SPILL, SPILL)

        def exchange_part(values):
            swapped = jnp.concatenate([values[1], values[0]], axis=1)
            come = lax.ppermute(swapped, "x", FLIP)
            return jnp.split(come, 2, axis=1)

        def lent(pack, value):
            quarter, come = weights[pack]
            value, come = tie(value, come)
            weights[pack] = natural(jnp.where(home, quarter, come))
            return value

        saved_list = []
        for layer in range(LAYERS):
            att_w = weights[3 * layer]
            out_w = [slot[:, 3 * local :] for slot in att_w]
            normed_one, hat_one, inv_one = norm_forward(
                stream, gains[layer, 0], shifts[layer, 0]
            )
            rows_one = both(normed_one.astype(jnp.bfloat16))
            biases = [qkv_bias(slot, layer) for slot in range(2)]
            qkv = [
                (
                    (product(rows_one, att_w[slot][:, : 3 * local], NN) + biases[slot])
                    * qkv_scale
                ).astype(jnp.bfloat16)
                for slot in range(2)
            ]
            halves = []
            for slot in range(2):
                rows = lax.dynamic_slice(qkv[slot], (part_start, 0), (PART, 3 * local))
                rows = rows.reshape(PART, pairs, 3 * LANES)[:, :, LANES:]
                halves.append(rows.reshape(PART, 2 * local))
            far = exchange_part(halves)
            mixed, lse_whole = attend_whole(place, qkv, pairs)
            far, mixed = tie(far, mixed)
            mixed_part, lse_part = attend_part(place, qkv, far, pairs)
            mixed = [
                lax.dynamic_update_slice(rows, part, (part_start, 0))
                for rows, part in zip(mixed, mixed_part)
            ]
            middle = stream + reduce_pair(mixed, out_w, NT) + shifts[layer, 1]
            normed_two, hat_two, inv_two = norm_forward(
                middle, gains[layer, 1], shifts[layer, 2]
            )
            rows_two = gather_quad(normed_two.astype(jnp.bfloat16))
            rows_two = lent(3 * layer + 1, rows_two)
            up_w = weights[3 * layer + 1]
            hidden = product(rows_two, up_w, NN) + up_bias[layer]
            activation = gelu_value(hidden).astype(jnp.bfloat16)
            if layer == LAYERS - 1:
                slope = gelu_slope(hidden).astype(jnp.bfloat16)
            else:
                (slope,) = tie(gelu_slope(tie(hidden)[0]).astype(jnp.bfloat16))
            activation = lent(3 * layer + 2, activation)
            down_w = weights[3 * layer + 2]
            if layer < LAYERS - 1:
                stream = middle + reduce_quad(activation, down_w, NT)
                stream = stream + shifts[layer, 3]
            saved_list.append(
                (
                    rows_one,
                    hat_one,
                    inv_one,
                    qkv,
                    far,
                    lse_whole,
                    lse_part,
                    mixed,
                    rows_two,
                    hat_two,
                    inv_two,
                    slope,
                    activation,
                )
            )
        token_grads, head_grads, unit_grads = ([None] * LAYERS for _ in range(3))
        streams = {}

        def advance_all(value, layer, phase):
            for stream in PHASES.get((layer, phase), ()):
                value = advance(value, streams[stream], core)
            return value

        for layer in reversed(range(LAYERS)):
            (
                rows_one,
                hat_one,
                inv_one,
                qkv,
                far,
                lse_whole,
                lse_part,
                mixed,
                rows_two,
                hat_two,
                inv_two,
                slope,
                activation,
            ) = saved_list[layer]
            att_w, up_w, down_w = weights[3 * layer : 3 * layer + 3]
            out_w = [slot[:, 3 * local :] for slot in att_w]
            shift_down = jnp.sum(cotangent, axis=0)
            if layer == LAYERS - 1:
                cot_rows = first_rows
            else:
                cot_rows = gather_quad(cotangent.astype(jnp.bfloat16))
            grad_hidden = product(cot_rows, down_w, NN) * slope.astype(jnp.float32)
            unit_grads[layer] = jnp.sum(grad_hidden, axis=0)
            hidden_rows = grad_hidden.astype(jnp.bfloat16)
            hidden_rows = advance_all(hidden_rows, layer, 0)
            back_two = reduce_quad(hidden_rows, up_w, NT)
            grad_down = natural(product(cot_rows, activation, TN).astype(jnp.bfloat16))
            grad_up = natural(product(rows_two, hidden_rows, TN).astype(jnp.bfloat16))
            streams["mlp", layer] = start_pair([grad_up, grad_down], home, 3 * layer + 1)
            back_two = advance_all(back_two, layer, 1)
            if layer == LAYERS - 1:
                back_two, last = tie(back_two, activation)
                stream = middle + reduce_quad(last, down_w, NT)
                every_out = share_rows(stream + shifts[layer, 3], home)
            dstream, gain_two, shift_two = norm_backward(
                back_two, gains[layer, 1], hat_two, inv_two
            )
            cotangent = cotangent + dstream
            shift_out = jnp.sum(cotangent, axis=0)
            cot_rows = both(cotangent.astype(jnp.bfloat16))
            grad_mixed = [
                product(cot_rows, out_w[slot], NN).astype(jnp.bfloat16) for slot in range(2)
            ]
            grad_out_w = [
                product(cot_rows, mixed[slot], TN).astype(jnp.bfloat16) for slot in range(2)
            ]
            grad_mixed = advance_all(grad_mixed, layer, 2)
            own_part, far_part, part_sums = back_part(place, qkv, far, grad_mixed, lse_part, pairs)
            grad_mixed, far_part = tie(grad_mixed, far_part)
            grad_mixed = advance_all(grad_mixed, layer, 3)
            come_part = exchange_part(far_part)
            grad_qkv, whole_sums = back_whole(place, qkv, grad_mixed, lse_whole, pairs)
            grad_qkv = advance_all(grad_qkv, layer, 4)
            sums = (part_sums + whole_sums)[:, :4].reshape(pairs, 2, 2, LANES)
            head_grads[layer] = [
                jnp.transpose(sums[:, slot], (1, 0, 2)).reshape(2, local) for slot in range(2)
            ]
            for slot in range(2):
                come = come_part[slot].astype(jnp.float32).reshape(PART, pairs, 2 * LANES)
                come = jnp.pad(come, ((0, 0), (0, 0), (LANES, 0))).reshape(PART, 3 * local)
                part = (own_part[slot] + come).astype(jnp.bfloat16)
                grad_qkv[slot] = lax.dynamic_update_slice(grad_qkv[slot], part, (part_start, 0))
            grad_att = [
                product(rows_one, grad_qkv[slot], TN).astype(jnp.bfloat16)
                for slot in range(2)
            ]
            grad_att = [
                natural(jnp.concatenate([grad_att[slot], grad_out_w[slot]], axis=1))
                for slot in range(2)
            ]
            streams["att", layer] = start_stream(grad_att, 3 * layer)
            qkv_w = [slot[:, : 3 * local] for slot in att_w]
            back_one = reduce_pair(grad_qkv, qkv_w, NT)
            back_one = advance_all(back_one, layer, 5)
            dstream, gain_one, shift_one = norm_backward(
                back_one, gains[layer, 0], hat_one, inv_one
            )
            cotangent = cotangent + dstream
            token_grads[layer] = (
                [gain_one, gain_two],
                [shift_one, shift_out, shift_two, shift_down],
            )
        cotangent = advance(cotangent, streams["att", 0], core)
        every_back = share_rows(cotangent, home)
        rows = [row for layer in range(LAYERS) for row in token_grads[layer][0]]
        rows += [row for layer in range(LAYERS) for row in token_grads[layer][1]]
        spots = [lax.broadcasted_iota(jnp.int32, (4, 1), 0) == quarter for quarter in quarters]
        for layer in range(LAYERS):
            for member in range(2):
                parts = [
                    jnp.where(spots[slot], head_grads[layer][slot][member][None], 0.0)
                    for slot in range(2)
                ]
                rows.append((parts[0] + parts[1]).reshape(-1))
        table = [jnp.stack(rows)]
        for layer in range(LAYERS):
            spot = lax.broadcasted_iota(jnp.int32, (4, 1), 0) == up_quarter
            table.append(jnp.where(spot, unit_grads[layer][None], 0.0))
        table = total_of(jnp.concatenate(table, axis=0))
        table = advance(table, streams["att", 0], core)
        for stream in streams.values():
            while stream["step"] < 3:
                advance((), stream, core)
        full_out = give_call(place, every_out)
        full_back = give_call(place, every_back)
        z = lax.axis_index("z")
        spot = 2 * z + core
        column = (4 * spot + 2 * y + x) * piece
        mine = lax.dynamic_slice(table, (0, column), (n_gain + n_bias, piece))
        grad_gain = mine[:n_gain].reshape(LAYERS, 2, piece)
        grad_shift = mine[n_gain:].reshape(LAYERS, 4, piece)
        base = n_gain + n_bias
        mine = table[base : base + 2 * LAYERS].reshape(2 * LAYERS, 4, heads, HEAD_DIM)
        mine = lax.dynamic_index_in_dim(mine, 2 * y + x, 1, keepdims=False)
        mine = lax.dynamic_slice_in_dim(mine, spot * f_head, f_head, 2)
        grad_qv = mine.reshape(b_qv.shape)
        mine = table[base + 2 * LAYERS :].reshape(LAYERS, 4, rows_up, -1)
        mine = lax.dynamic_index_in_dim(mine, 2 * y + x, 1, keepdims=False)
        grad_upb = lax.dynamic_slice_in_dim(mine, spot * f_up, f_up, 2)
        ended = {
            kind: [streams[kind, layer]["held"].astype(jnp.float32) for layer in range(LAYERS)]
            for kind in ("att", "mlp")
        }

        def unpack(grad):
            cols = grad[:, : 3 * local].reshape(-1, pairs, 3, LANES)
            return jnp.transpose(cols, (2, 0, 1, 3)).reshape(3, -1, local)

        return (
            full_out,
            full_back,
            jnp.stack([unpack(grad) for grad in ended["att"]]),
            grad_qv,
            jnp.stack([grad[:, 3 * local :].T for grad in ended["att"]]),
            jnp.stack([grad[:, :units] for grad in ended["mlp"]]),
            grad_upb,
            jnp.stack([grad[:, units:].T for grad in ended["mlp"]]),
            grad_gain,
            grad_shift,
        )

    return cells_step


def specs_for(images, group):
    both_axes = (*images, *group)
    rows = (
        P(images, None),
        P(images, None),
    )
    rest = (
        P(None, None, images, group),
        P(None, None, group, images),
        P(None, group, images),
        P(None, images, group),
        P(None, group, images),
        P(None, group, images),
        P(None, None, both_axes),
        P(None, None, both_axes),
    )
    return rows + rest


def solution(mesh):
    n_dp, n_tensor = mesh.shape["dp"], mesh.shape["tensor"]
    if n_tensor == 4 and n_dp % 2 == 0:
        sizes = (n_dp // 2, 2, 2, 2)
        cells = Mesh(mesh.devices.reshape(sizes), CELLS)
        specs = specs_for(("z", "core"), ("y", "x"))
        return jax.shard_map(
            cells_body(sizes), mesh=cells, in_specs=specs, out_specs=specs, check_vma=False
        )
    specs = specs_for(("dp",), ("tensor",))
    return jax.shard_map(shards, mesh=mesh, in_specs=specs, out_specs=specs, check_vma=False)
```

```python
import dataclasses
from typing import Any

import jax
import jax.numpy as jnp
import numpy as np
from jax import lax
from jax.experimental import pallas as pl
from jax.experimental.layout import Layout, with_layout_constraint
from jax.experimental.pallas import tpu as pltpu
from jax.sharding import Mesh
from jax.sharding import PartitionSpec as P

HEAD_DIM = 64
SEQ = 577
LAYERS = 2


epsilon = 1e-05
root_half = 0.7071067811865476
inv_root_two_pi = 0.3989422804014327


def norm_forward(stream_rows, gain_row, shift_row):
    center = stream_rows - jnp.mean(stream_rows, axis=-1, keepdims=True)
    inverse = lax.rsqrt(jnp.mean(center * center, axis=-1, keepdims=True) + epsilon)
    normed = center * inverse
    return (normed * gain_row + shift_row, normed, inverse)


def norm_backward(upstream, gain_row, normed, inverse):
    scaled = upstream * gain_row
    mean_one = jnp.mean(scaled, axis=-1, keepdims=True)
    mean_two = jnp.mean(scaled * normed, axis=-1, keepdims=True)
    return (
        inverse * (scaled - mean_one - normed * mean_two),
        jnp.sum(upstream * normed, axis=0),
        jnp.sum(upstream, axis=0),
    )


def gelu_value(hidden):
    return hidden * (0.5 * (1.0 + lax.erf(hidden * root_half)))


def gelu_slope(hidden):
    return (
        0.5 * (1.0 + lax.erf(hidden * root_half))
        + hidden * jnp.exp(-0.5 * hidden * hidden) * inv_root_two_pi
    )


def attend_image(inputs):
    query_rows, key_rows, value_rows = inputs
    scores = jnp.einsum("qhd,khd->hqk", query_rows, key_rows, preferred_element_type=jnp.float32)
    row_peak = jnp.max(scores, axis=-1, keepdims=True)
    exponent = jnp.exp(scores - row_peak)
    totals = jnp.sum(exponent, axis=-1, keepdims=True)
    attn_probs = (exponent / totals).astype(jnp.bfloat16)
    mixed_heads = jnp.einsum(
        "hqk,khd->qhd", attn_probs, value_rows, preferred_element_type=jnp.float32
    )
    return (mixed_heads.astype(jnp.bfloat16), (row_peak + jnp.log(totals))[..., 0])


def attend_back(inputs):
    query_rows, key_rows, value_rows, log_total, grad_mixed = inputs
    scores = jnp.einsum("qhd,khd->hqk", query_rows, key_rows, preferred_element_type=jnp.float32)
    attn_probs = jnp.exp(scores - log_total[..., None])
    grad_probs = jnp.einsum(
        "qhd,khd->hqk", grad_mixed, value_rows, preferred_element_type=jnp.float32
    )
    inner_sum = jnp.sum(attn_probs * grad_probs, axis=-1, keepdims=True)
    grad_scores = (attn_probs * (grad_probs - inner_sum)).astype(jnp.bfloat16)
    grad_query = jnp.einsum(
        "hqk,khd->qhd", grad_scores, key_rows, preferred_element_type=jnp.float32
    ) * HEAD_DIM ** (-0.5)
    grad_key = jnp.einsum(
        "hqk,qhd->khd", grad_scores, query_rows, preferred_element_type=jnp.float32
    )
    grad_value = jnp.einsum(
        "hqk,qhd->khd",
        attn_probs.astype(jnp.bfloat16),
        grad_mixed,
        preferred_element_type=jnp.float32,
    )
    return jnp.stack([grad_query, grad_key, grad_value], axis=1)


def fetch_forward(qkv_part, qv_part, out_part, up_part, upb_part, down_part):
    return (
        lax.all_gather(qkv_part, "dp", axis=1, tiled=True),
        lax.all_gather(qv_part, "dp", axis=2, tiled=True),
        lax.all_gather(out_part, "dp", axis=1, tiled=True),
        lax.all_gather(up_part, "dp", axis=0, tiled=True),
        lax.all_gather(upb_part, "dp", axis=1, tiled=True),
        lax.all_gather(down_part, "dp", axis=1, tiled=True),
    )


def fetch_again(qkv_part, qv_part, out_part, up_part, upb_part, down_part):
    return (
        lax.all_gather(qkv_part, "dp", axis=1, tiled=True),
        lax.all_gather(qv_part, "dp", axis=2, tiled=True),
        lax.all_gather(out_part, "dp", axis=1, tiled=True),
        lax.all_gather(up_part, "dp", axis=0, tiled=True),
        lax.all_gather(upb_part, "dp", axis=1, tiled=True),
        lax.all_gather(down_part, "dp", axis=1, tiled=True),
    )


def pad_rows(rows, extra_rows):
    return jnp.pad(rows, ((0, extra_rows), (0, 0)))


def spread_rows(token_rows, group_rows):
    return lax.all_gather(token_rows, "tensor", axis=0, tiled=True)[:group_rows]


def gather_cotangent(token_rows, group_rows):
    return lax.all_gather(token_rows, "tensor", axis=0, tiled=True)[:group_rows]


def reduce_branch(partial_rows, extra_rows):
    return lax.psum_scatter(
        pad_rows(partial_rows, extra_rows).astype(jnp.bfloat16),
        "tensor",
        scatter_dimension=0,
        tiled=True,
    ).astype(jnp.float32)


def branch_output(local_rows, local_w, extra_rows):
    return reduce_branch(
        jnp.dot(local_rows, local_w, preferred_element_type=jnp.float32), extra_rows
    )


def reduce_input(partial_rows, extra_rows):
    return lax.psum_scatter(
        pad_rows(partial_rows, extra_rows).astype(jnp.bfloat16),
        "tensor",
        scatter_dimension=0,
        tiled=True,
    ).astype(jnp.float32)


def reduce_weights(grad_qkvw, grad_qv, grad_outw, grad_up, grad_upb, grad_down):
    return (
        lax.psum_scatter(
            grad_qkvw.astype(jnp.bfloat16), "dp", scatter_dimension=1, tiled=True
        ).astype(jnp.float32),
        lax.psum_scatter(
            grad_qv.astype(jnp.bfloat16), "dp", scatter_dimension=2, tiled=True
        ).astype(jnp.float32),
        lax.psum_scatter(
            grad_outw.astype(jnp.bfloat16), "dp", scatter_dimension=1, tiled=True
        ).astype(jnp.float32),
        lax.psum_scatter(
            grad_up.astype(jnp.bfloat16), "dp", scatter_dimension=0, tiled=True
        ).astype(jnp.float32),
        lax.psum_scatter(
            grad_upb.astype(jnp.bfloat16), "dp", scatter_dimension=1, tiled=True
        ).astype(jnp.float32),
        lax.psum_scatter(
            grad_down.astype(jnp.bfloat16), "dp", scatter_dimension=1, tiled=True
        ).astype(jnp.float32),
    )


def shards(inputs, grad_out, w_qkv, b_qv, w_out, w_up, b_up, w_down, ln_gain, tok_bias):
    gains, shifts = (
        lax.all_gather(ln_gain, ("dp", "tensor"), axis=2, tiled=True),
        lax.all_gather(tok_bias, ("dp", "tensor"), axis=2, tiled=True),
    )
    score_scale = HEAD_DIM ** (-0.5)
    group_rows = inputs.shape[0]
    tensor_count = lax.axis_size("tensor")
    share_rows = (group_rows + tensor_count - 1) // tensor_count
    extra_rows = share_rows * tensor_count - group_rows
    row_offset = lax.axis_index("tensor") * share_rows
    images = group_rows // SEQ
    stream = lax.dynamic_slice_in_dim(pad_rows(inputs, extra_rows), row_offset, share_rows, 0)
    cotangent = lax.dynamic_slice_in_dim(pad_rows(grad_out, extra_rows), row_offset, share_rows, 0)
    saved_list = []
    for block_index in range(LAYERS):
        fetched = fetch_forward(
            w_qkv[block_index],
            b_qv[block_index],
            w_out[block_index],
            w_up[block_index],
            b_up[block_index],
            w_down[block_index],
        )
        qkv_w, qv_bias, out_w, up_w, up_bias, down_w = fetched
        local_width = qkv_w.shape[2]
        image_shape = (images, SEQ, local_width // HEAD_DIM, HEAD_DIM)
        normed_one, hat_one, inv_one = norm_forward(
            stream, gains[block_index, 0], shifts[block_index, 0]
        )
        rows_one = normed_one.astype(jnp.bfloat16)
        whole_one = spread_rows(rows_one, group_rows)
        projected = jnp.einsum("td,jde->tje", whole_one, qkv_w, preferred_element_type=jnp.float32)
        biases = qv_bias.reshape(2, local_width).astype(jnp.float32)
        query_rows = ((projected[:, 0] + biases[0]) * score_scale).astype(jnp.bfloat16)
        key_rows = projected[:, 1].astype(jnp.bfloat16)
        value_rows = (projected[:, 2] + biases[1]).astype(jnp.bfloat16)
        mixed_heads, log_total = lax.map(
            attend_image,
            (
                query_rows.reshape(image_shape),
                key_rows.reshape(image_shape),
                value_rows.reshape(image_shape),
            ),
        )
        mixed_heads = mixed_heads.reshape(-1, local_width)
        middle = stream + branch_output(mixed_heads, out_w, extra_rows) + shifts[block_index, 1]
        normed_two, hat_two, inv_two = norm_forward(
            middle, gains[block_index, 1], shifts[block_index, 2]
        )
        rows_two = normed_two.astype(jnp.bfloat16)
        whole_two = spread_rows(rows_two, group_rows)
        hidden = jnp.dot(whole_two, up_w, preferred_element_type=jnp.float32) + up_bias.reshape(
            -1
        ).astype(jnp.float32)
        activation = gelu_value(hidden).astype(jnp.bfloat16)
        stream = middle + branch_output(activation, down_w, extra_rows) + shifts[block_index, 3]
        saved_list.append(
            (
                fetched,
                rows_one,
                whole_one,
                hat_one,
                inv_one,
                query_rows,
                key_rows,
                value_rows,
                log_total,
                mixed_heads,
                rows_two,
                whole_two,
                hat_two,
                inv_two,
                hidden,
                activation,
            )
        )
    weight_list = [None] * LAYERS
    gain_list = [None] * LAYERS
    shift_list = [None] * LAYERS
    for block_index in reversed(range(LAYERS)):
        (
            fetched,
            rows_one,
            whole_one,
            hat_one,
            inv_one,
            query_rows,
            key_rows,
            value_rows,
            log_total,
            mixed_heads,
            rows_two,
            whole_two,
            hat_two,
            inv_two,
            hidden,
            activation,
        ) = saved_list[block_index]
        qkv_w, qv_bias, out_w, up_w, up_bias, down_w = fetch_again(
            w_qkv[block_index],
            b_qv[block_index],
            w_out[block_index],
            w_up[block_index],
            b_up[block_index],
            w_down[block_index],
        )
        local_width = qkv_w.shape[2]
        local_heads = local_width // HEAD_DIM
        image_shape = (images, SEQ, local_heads, HEAD_DIM)
        shift_down = jnp.sum(cotangent, axis=0)
        whole_cot = gather_cotangent(cotangent.astype(jnp.bfloat16), group_rows)
        grad_down = jnp.einsum(
            "tf,td->fd", activation, whole_cot, preferred_element_type=jnp.float32
        )
        grad_hidden = jnp.einsum(
            "td,fd->tf", whole_cot, down_w, preferred_element_type=jnp.float32
        ) * gelu_slope(hidden)
        grad_upb = jnp.sum(grad_hidden, axis=0)
        hidden_rows = grad_hidden.astype(jnp.bfloat16)
        grad_up = jnp.einsum(
            "td,tf->df", whole_two, hidden_rows, preferred_element_type=jnp.float32
        )
        back_two = reduce_input(
            jnp.einsum("tf,df->td", hidden_rows, up_w, preferred_element_type=jnp.float32),
            extra_rows,
        )
        dstream, gain_two, shift_two = norm_backward(
            back_two, gains[block_index, 1], hat_two, inv_two
        )
        cotangent = cotangent + dstream
        shift_out = jnp.sum(cotangent, axis=0)
        whole_cot = gather_cotangent(cotangent.astype(jnp.bfloat16), group_rows)
        grad_outw = jnp.einsum(
            "te,td->ed", mixed_heads, whole_cot, preferred_element_type=jnp.float32
        )
        grad_mixed = jnp.einsum(
            "td,ed->te", whole_cot, out_w, preferred_element_type=jnp.float32
        ).astype(jnp.bfloat16)
        qkv_grads = lax.map(
            attend_back,
            (
                query_rows.reshape(image_shape),
                key_rows.reshape(image_shape),
                value_rows.reshape(image_shape),
                log_total,
                grad_mixed.reshape(image_shape),
            ),
        )
        qkv_grads = qkv_grads.reshape(-1, 3, local_width)
        grad_qv = jnp.stack(
            [jnp.sum(qkv_grads[:, 0], axis=0), jnp.sum(qkv_grads[:, 2], axis=0)]
        ).reshape(2, local_heads, HEAD_DIM)
        qkv_rows = qkv_grads.astype(jnp.bfloat16)
        grad_qkvw = jnp.einsum(
            "td,tje->jde", whole_one, qkv_rows, preferred_element_type=jnp.float32
        )
        back_one = reduce_input(
            jnp.einsum("tje,jde->td", qkv_rows, qkv_w, preferred_element_type=jnp.float32),
            extra_rows,
        )
        dstream, gain_one, shift_one = norm_backward(
            back_one, gains[block_index, 0], hat_one, inv_one
        )
        cotangent = cotangent + dstream
        weight_list[block_index] = reduce_weights(
            grad_qkvw, grad_qv, grad_outw, grad_up, grad_upb.reshape(up_bias.shape), grad_down
        )
        gain_list[block_index] = jnp.stack([gain_one, gain_two])
        shift_list[block_index] = jnp.stack([shift_one, shift_out, shift_two, shift_down])
    gain_total, shift_total = (
        lax.psum_scatter(jnp.stack(gain_list), ("dp", "tensor"), scatter_dimension=2, tiled=True),
        lax.psum_scatter(jnp.stack(shift_list), ("dp", "tensor"), scatter_dimension=2, tiled=True),
    )
    full_out, full_back = (
        lax.all_gather(stream.astype(jnp.bfloat16), "tensor", axis=0, tiled=True).astype(
            stream.dtype
        ),
        lax.all_gather(cotangent.astype(jnp.bfloat16), "tensor", axis=0, tiled=True).astype(
            cotangent.dtype
        ),
    )
    stacked = [
        jnp.stack([weight_list[block_index][member] for block_index in range(LAYERS)])
        for member in range(6)
    ]
    return (
        full_out[:group_rows],
        full_back[:group_rows],
        stacked[0],
        stacked[1],
        stacked[2],
        stacked[3],
        stacked[4],
        stacked[5],
        gain_total,
        shift_total,
    )


ATT, MLP = range(2)


@dataclasses.dataclass
class Stream:
    grads: Any
    pack: int
    held: Any
    step: int
    home: Any


CELLS = ("z", "core", "y", "x")
PHASES = {
    (1, 4): ((MLP, 1),),
    (0, 1): ((ATT, 1),),
    (0, 4): ((ATT, 1), (MLP, 1)),
    (0, 5): ((MLP, 0),),
}
FLIP = ((0, 1), (1, 0))
TILE = 16
LANES = 128
NEGATIVE = -1e30
VMEM_LIMIT = 56 * 1024 * 1024


def round_up(count, multiple):
    return (count + multiple - 1) // multiple * multiple


WHOLE = round_up(SEQ, TILE)
PART_ROWS = (SEQ + 1) // 2
PART = round_up(PART_ROWS, TILE)
CHIP_ROWS = WHOLE + PART
SHARE = CHIP_ROWS // 2
SPILL = WHOLE - SHARE
NT = (((1,), (1,)), ((), ()))
TN = (((0,), (0,)), ((), ()))
NN = (((1,), (0,)), ((), ()))


def product(left, right, dims):
    return lax.dot_general(left, right, dims, preferred_element_type=jnp.float32)


def lane_pick(values, half):
    lane = lax.broadcasted_iota(jnp.int32, (1, values.shape[1]), 1)
    keep = lane < HEAD_DIM if half == 0 else lane >= HEAD_DIM
    return jnp.where(keep, values, jnp.zeros_like(values))


def whole_rows(ref, core):
    first = pl.multiple_of(core * SHARE, TILE)
    second = pl.multiple_of((1 - core) * SHARE, TILE)
    return jnp.concatenate([ref[pl.ds(first, SHARE), :], ref[pl.ds(second, SPILL), :]], axis=0)


def store_whole(ref, core, values, lanes):
    first = pl.multiple_of(core * SHARE, TILE)
    second = pl.multiple_of((1 - core) * SHARE, TILE)
    ref[pl.ds(first, SHARE), lanes] = values[:SHARE]
    ref[pl.ds(second, SPILL), lanes] = values[SHARE:]


def part_rows(ref, core):
    start = pl.multiple_of((1 - core) * SHARE + SPILL, TILE)
    return ref[pl.ds(start, PART), :]


def whole_keys():
    return lax.broadcasted_iota(jnp.int32, (WHOLE, 1), 0) < SEQ


def part_keys(mine):
    row = lax.broadcasted_iota(jnp.int32, (2 * PART, 1), 0)
    return (row < mine) | ((row >= PART) & (row < PART + SEQ - mine))


def attend_pair(query, key, value, good, lse_ref, slot):
    total = None
    for half in range(2):
        scores = product(lane_pick(key, half), query, NT)
        scores = jnp.where(good, scores, NEGATIVE)
        peak = jnp.max(scores, axis=0, keepdims=True)
        exponent = jnp.exp(scores - peak)
        sums = jnp.sum(exponent, axis=0, keepdims=True)
        probs = (exponent * (1.0 / sums)).astype(jnp.bfloat16)
        lse_ref[0, pl.ds(2 * slot + half, 1), :] = peak + jnp.log(sums)
        mixed = product(lane_pick(value, half), probs, TN)
        total = mixed if total is None else total + mixed
    return total.T.astype(jnp.bfloat16)


def attend_whole_kernel(place, qkv_a, qkv_b, mix_a, mix_b, lse_ref):
    core = place[0]
    good = whole_keys()
    for slot, (qkv, mix) in enumerate(((qkv_a, mix_a), (qkv_b, mix_b))):
        rows = whole_rows(qkv, core)
        mixed = attend_pair(
            rows[:, :LANES], rows[:, LANES : 2 * LANES], rows[:, 2 * LANES :], good, lse_ref, slot
        )
        store_whole(mix, core, mixed, slice(None))


def attend_part_kernel(place, qkv_a, qkv_b, far_a, far_b, mix_a, mix_b, lse_ref):
    core = place[0]
    good = part_keys(place[1])
    for slot, (qkv, far, mix) in enumerate(((qkv_a, far_a, mix_a), (qkv_b, far_b, mix_b))):
        rows = part_rows(qkv, core)
        key = jnp.concatenate([rows[:, LANES : 2 * LANES], far[:, :LANES]], axis=0)
        value = jnp.concatenate([rows[:, 2 * LANES :], far[:, LANES:]], axis=0)
        mix[...] = attend_pair(rows[:, :LANES], key, value, good, lse_ref, slot)


def attend_pair_back(query, key, value, upstream, good, lse_ref, slot):
    grad_key = grad_value = grad_query = None
    for half in range(2):
        lse = lse_ref[0, pl.ds(2 * slot + half, 1), :]
        key_half = lane_pick(key, half)
        scores = product(key_half, query, NT)
        probs = jnp.where(good, jnp.exp(scores - lse), 0.0)
        grad_probs = product(lane_pick(value, half), upstream, NT)
        inner = jnp.sum(probs * grad_probs, axis=0, keepdims=True)
        grad_scores = (probs * (grad_probs - inner)).astype(jnp.bfloat16)
        probs = probs.astype(jnp.bfloat16)
        some_key = product(grad_scores, lane_pick(query, half), NN)
        some_value = product(probs, lane_pick(upstream, half), NN)
        some_query = product(key_half, grad_scores, TN)
        grad_key = some_key if grad_key is None else grad_key + some_key
        grad_value = some_value if grad_value is None else grad_value + some_value
        grad_query = some_query if grad_query is None else grad_query + some_query
    return grad_query.T * HEAD_DIM ** (-0.5), grad_key, grad_value


def store_sums(sum_ref, slot, grad_query, grad_value):
    sum_ref[0, pl.ds(2 * slot, 1), :] = jnp.sum(grad_query, axis=0, keepdims=True)
    sum_ref[0, pl.ds(2 * slot + 1, 1), :] = jnp.sum(grad_value, axis=0, keepdims=True)


def back_whole_kernel(place, qkv_a, qkv_b, up_a, up_b, lse_ref, out_a, out_b, sum_ref):
    core = place[0]
    good = whole_keys()
    for slot, (qkv, up, out) in enumerate(((qkv_a, up_a, out_a), (qkv_b, up_b, out_b))):
        rows = whole_rows(qkv, core)
        grads = attend_pair_back(
            rows[:, :LANES],
            rows[:, LANES : 2 * LANES],
            rows[:, 2 * LANES :],
            whole_rows(up, core),
            good,
            lse_ref,
            slot,
        )
        store_sums(sum_ref, slot, grads[0], grads[2])
        for place_of, grad in enumerate(grads):
            lanes = slice(place_of * LANES, (place_of + 1) * LANES)
            store_whole(out, core, grad.astype(jnp.bfloat16), lanes)


def back_part_kernel(
    place, qkv_a, qkv_b, far_a, far_b, up_a, up_b, lse_ref, own_a, own_b, out_a, out_b, sum_ref
):
    core = place[0]
    good = part_keys(place[1])
    groups = ((qkv_a, far_a, up_a, own_a, out_a), (qkv_b, far_b, up_b, own_b, out_b))
    for slot, (qkv, far, up, own, out) in enumerate(groups):
        rows = part_rows(qkv, core)
        key = jnp.concatenate([rows[:, LANES : 2 * LANES], far[:, :LANES]], axis=0)
        value = jnp.concatenate([rows[:, 2 * LANES :], far[:, LANES:]], axis=0)
        grad_query, grad_key, grad_value = attend_pair_back(
            rows[:, :LANES], key, value, part_rows(up, core), good, lse_ref, slot
        )
        store_sums(sum_ref, slot, grad_query, grad_value)
        own[:, :LANES] = grad_query
        own[:, LANES : 2 * LANES] = grad_key[:PART]
        own[:, 2 * LANES :] = grad_value[:PART]
        out[:, :LANES] = grad_key[PART:].astype(jnp.bfloat16)
        out[:, LANES:] = grad_value[PART:].astype(jnp.bfloat16)


def by_pair(rows, lanes):
    return pl.BlockSpec((rows, lanes), lambda pair: (0, pair))


def stats(rows):
    return pl.BlockSpec((1, 8, rows), lambda pair: (pair, 0, 0))


def kernel_call(kernel, pairs, ins, in_specs, outs, out_specs):
    return pl.pallas_call(
kernel,
grid=(pairs,),
in_specs=[pl.BlockSpec(memory_space=pltpu.SMEM)] + in_specs,
out_specs=out_specs,
out_shape=[jax.ShapeDtypeStruct(shape, kind) for shape, kind in outs],
compiler_params=pltpu.CompilerParams(
    dimension_semantics=("arbitrary",), vmem_limit_bytes=VMEM_LIMIT
),
    )(*ins)


def attend_whole(place, qkv, pairs):
    mix = ((CHIP_ROWS, pairs * LANES), jnp.bfloat16)
    *mixed, lse = kernel_call(
        attend_whole_kernel,
        pairs,
        (place, *qkv),
        [by_pair(CHIP_ROWS, 3 * LANES)] * 2,
        [mix, mix, ((pairs, 8, WHOLE), jnp.float32)],
        [by_pair(CHIP_ROWS, LANES)] * 2 + [stats(WHOLE)],
    )
    return mixed, lse


def attend_part(place, qkv, far, pairs):
    mix = ((PART, pairs * LANES), jnp.bfloat16)
    *mixed, lse = kernel_call(
        attend_part_kernel,
        pairs,
        (place, *qkv, *far),
        [by_pair(CHIP_ROWS, 3 * LANES)] * 2 + [by_pair(PART, 2 * LANES)] * 2,
        [mix, mix, ((pairs, 8, PART), jnp.float32)],
        [by_pair(PART, LANES)] * 2 + [stats(PART)],
    )
    return mixed, lse


def back_whole(place, qkv, upstream, lse, pairs):
    out = ((CHIP_ROWS, 3 * pairs * LANES), jnp.bfloat16)
    *grads, sums = kernel_call(
        back_whole_kernel,
        pairs,
        (place, *qkv, *upstream, lse),
        [by_pair(CHIP_ROWS, 3 * LANES)] * 2
        + [by_pair(CHIP_ROWS, LANES)] * 2
        + [stats(WHOLE)],
        [out, out, ((pairs, 8, LANES), jnp.float32)],
        [by_pair(CHIP_ROWS, 3 * LANES)] * 2 + [stats(LANES)],
    )
    return grads, sums


def back_part(place, qkv, far, upstream, lse, pairs):
    own = ((PART, 3 * pairs * LANES), jnp.float32)
    out = ((PART, 2 * pairs * LANES), jnp.bfloat16)
    own_a, own_b, out_a, out_b, sums = kernel_call(
        back_part_kernel,
        pairs,
        (place, *qkv, *far, *upstream, lse),
        [by_pair(CHIP_ROWS, 3 * LANES)] * 2
        + [by_pair(PART, 2 * LANES)] * 2
        + [by_pair(CHIP_ROWS, LANES)] * 2
        + [stats(PART)],
        [own, own, out, out, ((pairs, 8, LANES), jnp.float32)],
        [by_pair(PART, 3 * LANES)] * 2 + [by_pair(PART, 2 * LANES)] * 2 + [stats(LANES)],
    )
    return (own_a, own_b), (out_a, out_b), sums


def give_kernel(place, round_00, round_01, round_10, round_11, out):
    y, x = place[2], place[3]
    near = [jnp.where(x == 0, a, b) for a, b in ((round_00[...], round_10[...]), (round_01[...], round_11[...]))]
    far = [jnp.where(x == 1, a, b) for a, b in ((round_00[...], round_10[...]), (round_01[...], round_11[...]))]
    row = 0
    tails = []
    for rounds in (near, far):
        whole = jnp.where(y == 0, rounds[0], rounds[1]).astype(jnp.float32)
        tail = jnp.where(y == 1, rounds[0], rounds[1]).astype(jnp.float32)
        out[row : row + SHARE, :] = whole
        out[row + SHARE : row + SEQ, :] = tail[: SEQ - SHARE]
        tails.append(tail)
        row += SEQ
    rest = SEQ - PART_ROWS
    out[row : row + PART_ROWS, :] = tails[0][SPILL : SPILL + PART_ROWS]
    out[row + PART_ROWS : row + SEQ, :] = tails[1][SPILL : SPILL + rest]


def give_call(place, rounds):
    width = rounds[0].shape[1]
    wide = 2 * LANES
    grid_spec = pltpu.PrefetchScalarGridSpec(
        num_scalar_prefetch=1,
        grid=(width // wide,),
        in_specs=[pl.BlockSpec((SHARE, wide), lambda col, place: (0, col))] * 4,
        out_specs=pl.BlockSpec((3 * SEQ, wide), lambda col, place: (0, col)),
    )
    return pl.pallas_call(
        give_kernel,
        grid_spec=grid_spec,
        out_shape=jax.ShapeDtypeStruct((3 * SEQ, width), jnp.float32),
        compiler_params=pltpu.CompilerParams(vmem_limit_bytes=VMEM_LIMIT),
    )(place, *rounds)


def natural(values):
    return with_layout_constraint(values, Layout((0, 1)))


def tie(*values):
    return lax.optimization_barrier(values)


def cell_moves(sizes, target):
    moves = []
    index = {cell: number for number, cell in enumerate(np.ndindex(*sizes))}
    for cell, number in index.items():
        goal = target(*cell)
        if goal is not None:
            moves.append((number, index[goal]))
    return moves


def cells_body(sizes):
    n_z, _, _, _ = sizes
    trade = cell_moves(
        sizes, lambda z, c, y, x: (z, c, y, 1 - x) if c == 0 else (z, c, 1 - y, x)
    )
    cross = cell_moves(
        sizes, lambda z, c, y, x: (z, c, y, 1 - x) if c == 1 else (z, c, 1 - y, x)
    )
    relay_y = cell_moves(
        sizes, lambda z, c, y, x: (z, 1, 1 - y, x) if c == 0 else (z, 0, y, x)
    )
    relay_x = cell_moves(sizes, lambda z, c, y, x: (z, 1, y, 1 - x) if c == 1 else None)
    back_y = cell_moves(
        sizes, lambda z, c, y, x: (z, 0, 1 - y, x) if c == 1 else (z, 1, y, x)
    )
    lend = cell_moves(
        sizes, lambda z, c, y, x: (z, c, 1 - y, x) if c == y else (z, 1 - c, y, x)
    )
    repay = cell_moves(
        sizes, lambda z, c, y, x: (z, c, 1 - y, x) if c != y else (z, 1 - c, y, x)
    )
    images_axis = ("z", "core")
    chips = ("y", "x")

    def move(values, moves):
        return lax.ppermute(values, CELLS, moves)

    def spread(quarter, core):
        half = quarter.shape[0] // 2
        slot_a = move(quarter, trade)
        upper = move(slot_a[:half], relay_y)
        lower = move(slot_a[half:], relay_x)
        slot_b = jnp.where(core == 0, quarter, jnp.concatenate([upper, lower], axis=0))
        return slot_a, natural(slot_b)

    def collect_far(grad_b):
        half = grad_b.shape[0] // 2
        return (move(grad_b[:half], back_y), move(grad_b[half:], relay_x))

    def collect_near(grad_a, come, core):
        half = grad_a.shape[0] // 2
        come = jnp.where(core == 0, come[0], come[1])
        piece = lax.dynamic_slice(grad_a, (core * half, 0), come.shape)
        piece = (piece.astype(jnp.float32) + come.astype(jnp.float32)).astype(jnp.bfloat16)
        grad_a = lax.dynamic_update_slice(grad_a, piece, (core * half, 0))
        return move(grad_a, trade)

    def collect_end(grad_b, traded, home):
        if isinstance(grad_b, list):
            mine = [
                jnp.where(home, kept.astype(jnp.float32) + come.astype(jnp.float32), 0.0)
                for kept, come in zip(grad_b, traded)
            ]
            mine = jnp.concatenate([part.astype(jnp.bfloat16) for part in mine], axis=1)
        else:
            kept = jnp.where(home, grad_b.astype(jnp.float32), 0.0)
            mine = (kept + traded.astype(jnp.float32)).astype(jnp.bfloat16)
        return natural(mine)

    def collect_sum(mine):
        return lax.psum_scatter(mine, images_axis, scatter_dimension=0, tiled=True)

    def start_stream(grads, pack):
        return Stream(grads, pack, collect_far(grads[1]), 0, None)

    def start_pair(grads, home, pack):
        held = [move(grad, repay) for grad in grads]
        return Stream((None, grads), pack, held, 1, home)

    def advance(value, stream, core):
        value, held = tie(value, stream.held)
        if stream.step == 0:
            held = collect_near(stream.grads[0], held, core)
        elif stream.step == 1:
            home = core == 0 if stream.home is None else stream.home
            value, held = tie(value, collect_end(stream.grads[1], held, home))
            held = collect_sum(held)
        stream.held, stream.step = held, stream.step + 1
        return value

    def gather_quad(values):
        across = lax.ppermute(values, "x", FLIP)
        near = flip(values)
        far = flip(across)
        return jnp.concatenate([values, near, across, far], axis=0)

    def reduce_quad(left, right, dims):
        far = product(left[3 * SHARE :], right, dims).astype(jnp.bfloat16)
        far = flip(far)
        across = product(left[2 * SHARE : 3 * SHARE], right, dims)
        across = (across + far.astype(jnp.float32)).astype(jnp.bfloat16)
        across = lax.ppermute(across, "x", FLIP)
        near = product(left[SHARE : 2 * SHARE], right, dims).astype(jnp.bfloat16)
        near = flip(near)
        own = product(left[:SHARE], right, dims)
        return own + near.astype(jnp.float32) + across.astype(jnp.float32)

    def total_of(table):
        come = flip(table)
        table = table + come
        table = table + move(table, cross)
        table = flip(table)
        table = table + move(table, cross)
        gap = 1
        while gap < n_z:
            if n_z % (2 * gap):
                return lax.psum(table, CELLS[0])
            partner = [(z, z ^ gap) for z in range(n_z)]
            table = table + lax.ppermute(table, CELLS[0], partner)
            gap *= 2
        return table

    def flip(values):
        return lax.ppermute(values, "core", FLIP)

    def both(values):
        return jnp.concatenate([values, flip(values)], axis=0)

    def reduce_pair(lefts, rights, dims):
        other = sum(
            product(left[SHARE:], right, dims) for left, right in zip(lefts, rights)
        )
        other = flip(other.astype(jnp.bfloat16))
        own = sum(product(left[:SHARE], right, dims) for left, right in zip(lefts, rights))
        return own + other.astype(jnp.float32)

    def share_of(rows, x, part):
        width = rows.shape[1]
        if part == 0:
            return lax.dynamic_slice(rows, (SEQ * x, 0), (SHARE, width))
        tail = lax.dynamic_slice(rows, (SEQ * x + SHARE, 0), (SEQ - SHARE, width))
        split = lax.dynamic_slice(
            rows, (2 * SEQ + PART_ROWS * x, 0), (SEQ - PART_ROWS, width)
        )
        last = rows[2 * SEQ + PART_ROWS - 1 : 2 * SEQ + PART_ROWS]
        last = jnp.where(x == 0, last, jnp.zeros_like(last))
        return jnp.concatenate(
            [
                tail,
                jnp.zeros((WHOLE - SEQ, width), rows.dtype),
                split,
                last,
                jnp.zeros((PART - PART_ROWS, width), rows.dtype),
            ],
            axis=0,
        )

    def take_share(rows, core, y, x):
        shares = share_of(rows, x, 0), share_of(rows, x, 1)
        own = jnp.where(core == 0, shares[0], shares[1])
        come = flip(jnp.where(core == 0, shares[1], shares[0]))
        return jnp.where(core == y, own, come)

    def share_rows(share, home):
        share = share.astype(jnp.bfloat16)
        rounds = []
        for number in range(4):
            dx, dc = divmod(number, 2)
            moves = cell_moves(
                sizes, lambda z, c, y, x, dx=dx, dc=dc: (z, y, c ^ dc, x ^ dx)
            )
            moves = [(a, b) for a, b in moves if a != b]
            come = move(share, moves)
            rounds.append(jnp.where(home, share, come) if number == 0 else come)
        return rounds

    def cells_step(inputs, grad_out, w_qkv, b_qv, w_out, w_up, b_up, w_down, ln_gain, tok_bias):
        core, y, x = (lax.axis_index(name) for name in ("core", "y", "x"))
        quarter_a = jnp.where(core == 0, 2 * y + 1 - x, 2 * (1 - y) + x)
        quarter_b = jnp.where(core == 0, 2 * y + x, 2 * (1 - y) + 1 - x)
        quarters = (quarter_a, quarter_b)
        place = jnp.stack([core, PART_ROWS - x, y, x]).astype(jnp.int32)
        width = inputs.shape[1]
        heads = b_qv.shape[2]
        local = heads * HEAD_DIM
        pairs = local // LANES
        units = w_up.shape[2]
        n_dp = 2 * n_z
        n_dev = 4 * n_dp
        piece = width // n_dev

        def pack_attention(layer):
            cols = [
                w_qkv[layer, member][:, pair * LANES : (pair + 1) * LANES]
                for pair in range(pairs)
                for member in range(3)
            ]
            return jnp.concatenate(cols + [w_out[layer].T], axis=1)

        packs = []
        for layer in range(LAYERS):
            packs += [pack_attention(layer), w_up[layer], w_down[layer].T]
        whole = []
        for pack in packs:
            whole.append(natural(lax.all_gather(natural(pack), images_axis, axis=0, tiled=True)))
        home = core == y
        weights = []
        for pack, quarter in enumerate(whole):
            if pack % 3 == 0:
                weights.append(spread(quarter, core))
            else:
                weights.append((quarter, move(quarter, lend)))

        small = jnp.concatenate(
            [
                ln_gain.reshape(-1, piece),
                tok_bias.reshape(-1, piece),
                b_qv.astype(jnp.float32).reshape(-1, piece),
                b_up.astype(jnp.float32).reshape(-1, piece),
            ],
            axis=0,
        )
        n_gain, n_bias, n_qv = 2 * LAYERS, 4 * LAYERS, b_qv.size // piece
        table = lax.all_gather(small, images_axis, axis=0)
        table = lax.all_gather(table, chips, axis=0)
        inputs, table, _ = tie(inputs, table, whole[0])
        stream = take_share(inputs, core, y, x)
        tokens = jnp.transpose(table[:, :, : n_gain + n_bias], (2, 1, 0, 3)).reshape(-1, width)
        gains = tokens[:n_gain].reshape(LAYERS, 2, width)
        shifts = tokens[n_gain:].reshape(LAYERS, 4, width)
        f_head = b_qv.shape[3]
        rows_up, f_up = b_up.shape[1], b_up.shape[2]
        head_bias = []
        for quarter in quarters:
            mine = lax.dynamic_index_in_dim(table, quarter, 0, keepdims=False)
            part = mine[:, n_gain + n_bias : n_gain + n_bias + n_qv]
            part = part.reshape(n_dp, LAYERS, 2, heads, f_head)
            head_bias.append(jnp.transpose(part, (1, 2, 3, 0, 4)).reshape(LAYERS, 2, local))
        up_quarter = 2 * core + x
        mine = lax.dynamic_index_in_dim(table, up_quarter, 0, keepdims=False)
        part = mine[:, n_gain + n_bias + n_qv :].reshape(n_dp, LAYERS, rows_up, f_up)
        up_bias = jnp.transpose(part, (1, 2, 0, 3)).reshape(LAYERS, 1, units)

        def qkv_bias(slot, layer):
            rows = head_bias[slot][layer].reshape(2, pairs, LANES)
            zero = jnp.zeros_like(rows[0])
            return jnp.stack([rows[0], zero, rows[1]], axis=1).reshape(1, -1)

        unit = jnp.ones((LANES,), jnp.float32)
        qkv_scale = jnp.tile(jnp.concatenate([unit * HEAD_DIM ** (-0.5), unit, unit]), pairs)
        part_start = jnp.where(core == 0, SHARE + SPILL, SPILL)

        def exchange_part(values):
            swapped = jnp.concatenate([values[1], values[0]], axis=1)
            come = lax.ppermute(swapped, "x", FLIP)
            return jnp.split(come, 2, axis=1)

        def lent(pack, value):
            quarter, come = weights[pack]
            value, come = tie(value, come)
            weights[pack] = natural(jnp.where(home, quarter, come))
            return value

        saved_list = []
        for layer in range(LAYERS):
            att_w = weights[3 * layer]
            out_w = [slot[:, 3 * local :] for slot in att_w]
            normed_one, hat_one, inv_one = norm_forward(
                stream, gains[layer, 0], shifts[layer, 0]
            )
            rows_one = both(normed_one.astype(jnp.bfloat16))
            biases = [qkv_bias(slot, layer) for slot in range(2)]
            qkv = [
                (
                    (product(rows_one, att_w[slot][:, : 3 * local], NN) + biases[slot])
                    * qkv_scale
                ).astype(jnp.bfloat16)
                for slot in range(2)
            ]
            halves = []
            for slot in range(2):
                rows = lax.dynamic_slice(qkv[slot], (part_start, 0), (PART, 3 * local))
                rows = rows.reshape(PART, pairs, 3 * LANES)[:, :, LANES:]
                halves.append(rows.reshape(PART, 2 * local))
            far = exchange_part(halves)
            mixed, lse_whole = attend_whole(place, qkv, pairs)
            far, mixed = tie(far, mixed)
            mixed_part, lse_part = attend_part(place, qkv, far, pairs)
            mixed = [
                lax.dynamic_update_slice(rows, part, (part_start, 0))
                for rows, part in zip(mixed, mixed_part)
            ]
            middle = stream + reduce_pair(mixed, out_w, NT) + shifts[layer, 1]
            normed_two, hat_two, inv_two = norm_forward(
                middle, gains[layer, 1], shifts[layer, 2]
            )
            rows_two = gather_quad(normed_two.astype(jnp.bfloat16))
            if layer == 0:
                cotangent, normed_two = tie(grad_out, normed_two)
                cotangent = take_share(cotangent, core, y, x)
                rows_two, cotangent = tie(rows_two, cotangent)
                first_rows = gather_quad(cotangent.astype(jnp.bfloat16))
            rows_two = lent(3 * layer + 1, rows_two)
            up_w = weights[3 * layer + 1]
            hidden = product(rows_two, up_w, NN) + up_bias[layer]
            activation = gelu_value(hidden).astype(jnp.bfloat16)
            if layer == LAYERS - 1:
                slope = gelu_slope(hidden).astype(jnp.bfloat16)
            else:
                (slope,) = tie(gelu_slope(tie(hidden)[0]).astype(jnp.bfloat16))
            activation = lent(3 * layer + 2, activation)
            down_w = weights[3 * layer + 2]
            if layer < LAYERS - 1:
                stream = middle + reduce_quad(activation, down_w, NT)
                stream = stream + shifts[layer, 3]
            saved_list.append(
                (
                    rows_one,
                    hat_one,
                    inv_one,
                    qkv,
                    far,
                    lse_whole,
                    lse_part,
                    mixed,
                    rows_two,
                    hat_two,
                    inv_two,
                    slope,
                    activation,
                )
            )
        token_grads, head_grads, unit_grads = ([None] * LAYERS for _ in range(3))
        streams = {}

        def advance_all(value, layer, phase):
            for stream in PHASES.get((layer, phase), ()):
                value = advance(value, streams[stream], core)
            return value

        for layer in reversed(range(LAYERS)):
            (
                rows_one,
                hat_one,
                inv_one,
                qkv,
                far,
                lse_whole,
                lse_part,
                mixed,
                rows_two,
                hat_two,
                inv_two,
                slope,
                activation,
            ) = saved_list[layer]
            att_w, up_w, down_w = weights[3 * layer : 3 * layer + 3]
            out_w = [slot[:, 3 * local :] for slot in att_w]
            shift_down = jnp.sum(cotangent, axis=0)
            if layer == LAYERS - 1:
                cot_rows = first_rows
            else:
                cot_rows = gather_quad(cotangent.astype(jnp.bfloat16))
            grad_hidden = product(cot_rows, down_w, NN) * slope.astype(jnp.float32)
            unit_grads[layer] = jnp.sum(grad_hidden, axis=0)
            hidden_rows = grad_hidden.astype(jnp.bfloat16)
            hidden_rows = advance_all(hidden_rows, layer, 0)
            back_two = reduce_quad(hidden_rows, up_w, NT)
            grad_down = natural(product(cot_rows, activation, TN).astype(jnp.bfloat16))
            grad_up = natural(product(rows_two, hidden_rows, TN).astype(jnp.bfloat16))
            streams[MLP, layer] = start_pair([grad_up, grad_down], home, 3 * layer + 1)
            back_two = advance_all(back_two, layer, 1)
            if layer == LAYERS - 1:
                back_two, last = tie(back_two, activation)
                stream = middle + reduce_quad(last, down_w, NT)
                every_out = share_rows(stream + shifts[layer, 3], home)
            dstream, gain_two, shift_two = norm_backward(
                back_two, gains[layer, 1], hat_two, inv_two
            )
            cotangent = cotangent + dstream
            shift_out = jnp.sum(cotangent, axis=0)
            cot_rows = both(cotangent.astype(jnp.bfloat16))
            grad_mixed = [
                product(cot_rows, out_w[slot], NN).astype(jnp.bfloat16) for slot in range(2)
            ]
            grad_out_w = [
                product(cot_rows, mixed[slot], TN).astype(jnp.bfloat16) for slot in range(2)
            ]
            grad_mixed = advance_all(grad_mixed, layer, 2)
            own_part, far_part, part_sums = back_part(place, qkv, far, grad_mixed, lse_part, pairs)
            grad_mixed, far_part = tie(grad_mixed, far_part)
            grad_mixed = advance_all(grad_mixed, layer, 3)
            come_part = exchange_part(far_part)
            grad_qkv, whole_sums = back_whole(place, qkv, grad_mixed, lse_whole, pairs)
            grad_qkv = advance_all(grad_qkv, layer, 4)
            sums = (part_sums + whole_sums)[:, :4].reshape(pairs, 2, 2, LANES)
            head_grads[layer] = [
                jnp.transpose(sums[:, slot], (1, 0, 2)).reshape(2, local) for slot in range(2)
            ]
            for slot in range(2):
                come = come_part[slot].astype(jnp.float32).reshape(PART, pairs, 2 * LANES)
                come = jnp.pad(come, ((0, 0), (0, 0), (LANES, 0))).reshape(PART, 3 * local)
                part = (own_part[slot] + come).astype(jnp.bfloat16)
                grad_qkv[slot] = lax.dynamic_update_slice(grad_qkv[slot], part, (part_start, 0))
            grad_att = [
                product(rows_one, grad_qkv[slot], TN).astype(jnp.bfloat16)
                for slot in range(2)
            ]
            grad_att = [
                natural(jnp.concatenate([grad_att[slot], grad_out_w[slot]], axis=1))
                for slot in range(2)
            ]
            streams[ATT, layer] = start_stream(grad_att, 3 * layer)
            qkv_w = [slot[:, : 3 * local] for slot in att_w]
            back_one = reduce_pair(grad_qkv, qkv_w, NT)
            back_one = advance_all(back_one, layer, 5)
            dstream, gain_one, shift_one = norm_backward(
                back_one, gains[layer, 0], hat_one, inv_one
            )
            cotangent = cotangent + dstream
            token_grads[layer] = (
                [gain_one, gain_two],
                [shift_one, shift_out, shift_two, shift_down],
            )
        cotangent = advance(cotangent, streams[ATT, 0], core)
        every_back = share_rows(cotangent, home)
        rows = [row for layer in range(LAYERS) for row in token_grads[layer][0]]
        rows += [row for layer in range(LAYERS) for row in token_grads[layer][1]]
        spots = [lax.broadcasted_iota(jnp.int32, (4, 1), 0) == quarter for quarter in quarters]
        for layer in range(LAYERS):
            for member in range(2):
                parts = [
                    jnp.where(spots[slot], head_grads[layer][slot][member][None], 0.0)
                    for slot in range(2)
                ]
                rows.append((parts[0] + parts[1]).reshape(-1))
        table = [jnp.stack(rows)]
        for layer in range(LAYERS):
            spot = lax.broadcasted_iota(jnp.int32, (4, 1), 0) == up_quarter
            table.append(jnp.where(spot, unit_grads[layer][None], 0.0))
        table = total_of(jnp.concatenate(table, axis=0))
        table = advance(table, streams[ATT, 0], core)
        full_out = give_call(place, every_out)
        for stream in streams.values():
            while stream.step < 3:
                advance((), stream, core)
        full_back = give_call(place, every_back)
        z = lax.axis_index("z")
        spot = 2 * z + core
        column = (4 * spot + 2 * y + x) * piece
        mine = lax.dynamic_slice(table, (0, column), (n_gain + n_bias, piece))
        grad_gain = mine[:n_gain].reshape(LAYERS, 2, piece)
        grad_shift = mine[n_gain:].reshape(LAYERS, 4, piece)
        base = n_gain + n_bias
        mine = table[base : base + 2 * LAYERS].reshape(2 * LAYERS, 4, heads, HEAD_DIM)
        mine = lax.dynamic_index_in_dim(mine, 2 * y + x, 1, keepdims=False)
        mine = lax.dynamic_slice_in_dim(mine, spot * f_head, f_head, 2)
        grad_qv = mine.reshape(b_qv.shape)
        mine = table[base + 2 * LAYERS :].reshape(LAYERS, 4, rows_up, -1)
        mine = lax.dynamic_index_in_dim(mine, 2 * y + x, 1, keepdims=False)
        grad_upb = lax.dynamic_slice_in_dim(mine, spot * f_up, f_up, 2)
        ended = {
            kind: [streams[kind, layer].held.astype(jnp.float32) for layer in range(LAYERS)]
            for kind in (ATT, MLP)
        }

        def unpack(grad):
            cols = grad[:, : 3 * local].reshape(-1, pairs, 3, LANES)
            return jnp.transpose(cols, (2, 0, 1, 3)).reshape(3, -1, local)

        return (
            full_out,
            full_back,
            jnp.stack([unpack(grad) for grad in ended[ATT]]),
            grad_qv,
            jnp.stack([grad[:, 3 * local :].T for grad in ended[ATT]]),
            jnp.stack([grad[:, :units] for grad in ended[MLP]]),
            grad_upb,
            jnp.stack([grad[:, units:].T for grad in ended[MLP]]),
            grad_gain,
            grad_shift,
        )

    return cells_step


def specs_for(images, group):
    both_axes = (*images, *group)
    rows = (
        P(images, None),
        P(images, None),
    )
    rest = (
        P(None, None, images, group),
        P(None, None, group, images),
        P(None, group, images),
        P(None, images, group),
        P(None, group, images),
        P(None, group, images),
        P(None, None, both_axes),
        P(None, None, both_axes),
    )
    return rows + rest


def solution(mesh):
    n_dp, n_tensor = mesh.shape["dp"], mesh.shape["tensor"]
    if n_tensor == 4 and n_dp % 2 == 0:
        sizes = (n_dp // 2, 2, 2, 2)
        cells = Mesh(mesh.devices.reshape(sizes), CELLS)
        specs = specs_for(("z", "core"), ("y", "x"))
        return jax.shard_map(
            cells_body(sizes), mesh=cells, in_specs=specs, out_specs=specs, check_vma=False
        )
    specs = specs_for(("dp",), ("tensor",))
    return jax.shard_map(shards, mesh=mesh, in_specs=specs, out_specs=specs, check_vma=False)
```
